32 devices in a mesh: space: 2 (over x), mom: 16 (over z, y, core).
Axes of the slice: x: 2, y: 2, z: 4, core: 2. Of those that a mesh axis runs over, the one named last changes fastest.
Arguments:
- distribution: float32 [8, 16, 8, 1024], P('space', 'mom'), may hold values from 0.1 to 2
- a_factor: bfloat16 [1024, 8192], P(None, 'mom'), may hold values from -0.1875 to 0.1875
- b_factor: bfloat16 [1024, 8192], P(None, 'mom'), may hold values from -0.1875 to 0.1875
- velocity: float32 [3, 1024], replicated, may hold values from -1 to 1
- drift: float32 [1024], replicated, may hold values from 0.05 to 0.5
Outputs:
- distribution_out: float32 [8, 16, 8, 1024], P('space', 'mom')
The draws below stay inside these ranges and needn't reach their ends.
All inputs are finite; a program needn't handle non-finite values.
Results may differ from the reference program's by a relative error of at most 0.001.
Values may be sent and summed in bfloat16 or wider, within the bound.
No kernel may reach another device: no remote copies, remote signals or barrier semaphores. Data moves between devices by JAX's collectives and lax.ppermute only.
A program may use at most 64 MiB of HBM per device.

```python
import math
import jax
import jax.numpy as jnp
from jax import lax

NZ = 8
P_SIZE = 1024
RANK = 8
NDIR = 16
ITERS = 2
NX = 8
NY = 16


def level_of(key, extent, split, low, top_value):
    level = 1.0
    for axis_at, shards_of in split:
        steps = jax.random.uniform(jax.random.fold_in(jax.random.fold_in(key, 6), axis_at), (shards_of,), jnp.float32, low / len(split), top_value / len(split))
        level = level * jnp.repeat(jnp.exp(steps), extent[axis_at] // shards_of).reshape((-1,) + (1,) * (len(extent) - 1 - axis_at))
    return level


def normal_values(key, extent, scale, bound, shards=(), kind=jnp.bfloat16):
    level = level_of(key, extent, shards, -0.22, 0.18) if shards else 1.0
    result = jax.random.normal(key, extent, jnp.float32) * scale * level
    return jnp.minimum(jnp.maximum(result, -bound), bound).astype(kind)


def setup_inputs(seed: int = 0) -> dict:
    streams_of = jax.random.split(jax.random.key(seed), 6)
    return {
        "distribution": jnp.clip(jnp.exp(math.log(2.0) - 2.9957323 * jax.random.uniform(streams_of[0], (NX, NY, NZ, P_SIZE), jnp.float32) ** level_of(streams_of[0], (NX, NY, NZ, P_SIZE), ((0, 2), (1, 16)), -0.2, 0.2)), 0.1, 2.0),
        "a_factor": normal_values(streams_of[1], (P_SIZE, P_SIZE * RANK), P_SIZE ** -0.5, 0.1875, ((1, 16),)),
        "b_factor": normal_values(streams_of[2], (P_SIZE, P_SIZE * RANK), P_SIZE ** -0.5, 0.1875, ((1, 16),)),
        "velocity": jnp.clip(jax.random.uniform(streams_of[3], (3, P_SIZE), jnp.float32, -1.0, 1.0), -1.0, 1.0),
        "drift": jnp.clip(jnp.exp(jax.random.uniform(streams_of[4], (P_SIZE,), jnp.float32, math.log(0.05), math.log(0.5))), 0.05, 0.5),
    }


collide_rate = 0.1
courant = 0.3


def collide(state, a_factor, b_factor):
    def one_plane(plane):
        rows_flat = plane.reshape(NY * NZ, P_SIZE).astype(jnp.bfloat16)
        proj_a = jnp.dot(rows_flat, a_factor, preferred_element_type=jnp.float32)
        proj_b = jnp.dot(rows_flat, b_factor, preferred_element_type=jnp.float32)
        summed = (proj_a * proj_b).reshape(NY * NZ, P_SIZE, RANK).sum(axis=2)
        return summed.reshape(NY, NZ, P_SIZE)

    return lax.map(one_plane, state)


def upwind(center, behind, beyond, speeds):
    return jnp.maximum(speeds, 0.0) * (center - behind) + jnp.minimum(speeds, 0.0) * (beyond - center)


def reference(distribution, a_factor, b_factor, velocity, drift):
    state = distribution
    for substep in range(ITERS):
        collided = state + collide_rate * collide(state, a_factor, b_factor)
        read = collided
        for dim_index in range(3):
            behind = jnp.roll(collided, 1, axis=dim_index)
            beyond = jnp.roll(collided, -1, axis=dim_index)
            read = read - courant * upwind(collided, behind, beyond, velocity[dim_index])
        upper = jnp.concatenate([read[..., NDIR:], jnp.zeros(read.shape[:3] + (NDIR,), jnp.float32)], axis=3)
        state = read + drift * (upper - read)
    return state
```

```python
import jax
import jax.numpy as jnp
from jax import lax
from jax.sharding import PartitionSpec as P

P_SIZE = 1024
RANK = 8
NDIR = 16
ITERS = 2


collide_rate = 0.1
courant = 0.3


def swap(block, axis, bits):
    count = lax.axis_size(axis)
    return lax.ppermute(block, axis, [(i, i ^ bits) for i in range(count)])


def gathered(own, axis):
    count = lax.axis_size(axis)
    if count % 4 or count & (count - 1):
        return lax.all_gather(own, axis, axis=0, tiled=False)
    me = lax.axis_index(axis)
    blocks = {0: own}
    for bits in range(4, count, 4):
        blocks[bits] = swap(own, axis, bits)
    for bits in range(0, count, 4):
        blocks[bits ^ 2] = swap(blocks[bits], axis, 2)
    even = jnp.stack([blocks[bits] for bits in range(0, count, 2)])
    odd = swap(even, axis, 1)
    whole = jnp.zeros((count,) + own.shape, own.dtype)
    for at in range(count // 2):
        whole = lax.dynamic_update_index_in_dim(whole, even[at], me ^ (2 * at), 0)
        whole = lax.dynamic_update_index_in_dim(whole, odd[at], me ^ (2 * at) ^ 1, 0)
    return whole


def halo(cells, axis, dim, dtype):
    count = lax.axis_size(axis)
    size = cells.shape[dim]
    head = lax.slice_in_dim(cells, 0, 1, axis=dim).astype(dtype)
    tail = lax.slice_in_dim(cells, size - 1, size, axis=dim).astype(dtype)
    if count == 2:
        both = swap(jnp.concatenate([tail, head], axis=dim), axis, 1)
        behind = lax.slice_in_dim(both, 0, 1, axis=dim)
        ahead = lax.slice_in_dim(both, 1, 2, axis=dim)
    elif count % 2 == 0:
        odd = lax.axis_index(axis) % 2 == 1
        near = swap(jnp.where(odd, head, tail), axis, 1)
        pairs = [(i, (i + 1) % count if i % 2 else (i - 1) % count) for i in range(count)]
        far = lax.ppermute(jnp.where(odd, tail, head), axis, pairs)
        behind = jnp.where(odd, near, far)
        ahead = jnp.where(odd, far, near)
    else:
        behind = lax.ppermute(tail, axis, [(i, (i + 1) % count) for i in range(count)])
        ahead = lax.ppermute(head, axis, [((i + 1) % count, i) for i in range(count)])
    return behind.astype(cells.dtype), ahead.astype(cells.dtype)


def shifted(cells, behind, ahead, dim):
    size = cells.shape[dim]
    back = jnp.concatenate([behind, lax.slice_in_dim(cells, 0, size - 1, axis=dim)], axis=dim)
    forth = jnp.concatenate([lax.slice_in_dim(cells, 1, size, axis=dim), ahead], axis=dim)
    return back, forth


def upwind(center, behind, beyond, speeds):
    return jnp.maximum(speeds, 0.0) * (center - behind) + jnp.minimum(speeds, 0.0) * (
        beyond - center
    )


def rank_sum(proj_a, proj_b, width):
    return (proj_a * proj_b).reshape(proj_a.shape[0], width, RANK).sum(axis=2)


def per_device(distribution, a_factor, b_factor, velocity, drift):
    width = a_factor.shape[1] // RANK
    state = distribution
    for substep in range(ITERS):
        piece = gathered(state.astype(jnp.bfloat16), "mom")
        rows_flat = piece.reshape(-1, P_SIZE)
        proj_a = jnp.dot(rows_flat, a_factor, preferred_element_type=jnp.float32)
        proj_b = jnp.dot(rows_flat, b_factor, preferred_element_type=jnp.float32)
        summed = rank_sum(proj_a, proj_b, width)
        terms = summed.reshape(piece.shape[:4] + (width,)).astype(jnp.bfloat16)
        collision = lax.all_to_all(terms, "mom", split_axis=0, concat_axis=0, tiled=True)
        collision = jnp.moveaxis(collision, 0, 3).reshape(state.shape).astype(jnp.float32)
        collided = state + collide_rate * collision
        x_behind, x_ahead = halo(collided, "space", 0, jnp.bfloat16)
        y_behind, y_ahead = halo(collided, "mom", 1, jnp.bfloat16)
        read = collided - courant * upwind(
            collided, *shifted(collided, x_behind, x_ahead, 0), velocity[0]
        )
        read = read - courant * upwind(
            collided, *shifted(collided, y_behind, y_ahead, 1), velocity[1]
        )
        read = read - courant * upwind(
            collided, jnp.roll(collided, 1, axis=2), jnp.roll(collided, -1, axis=2), velocity[2]
        )
        upper = jnp.concatenate(
            [read[..., NDIR:], jnp.zeros(read.shape[:3] + (NDIR,), jnp.float32)], axis=3
        )
        state = read + drift * (upper - read)
    return state


def solution(mesh):
    in_specs = (P("space", "mom", None, None), P(None, "mom"), P(None, "mom"), P(), P())
    out_specs = P("space", "mom", None, None)
    return jax.shard_map(
        per_device, mesh=mesh, in_specs=in_specs, out_specs=out_specs, check_vma=False
    )
```

```python
import functools

import jax
import jax.numpy as jnp
from jax import lax
from jax.experimental import pallas as pl
from jax.experimental.pallas import tpu as pltpu
from jax.sharding import PartitionSpec as P

P_SIZE = 1024
RANK = 8
NDIR = 16
ITERS = 2


collide_rate = 0.1
courant = 0.3


def swap(block, axis, bits):
    count = lax.axis_size(axis)
    return lax.ppermute(block, axis, [(i, i ^ bits) for i in range(count)])


def gathered(own, axis):
    count = lax.axis_size(axis)
    blocks = {0: own}
    for bits in range(4, count, 4):
        blocks[bits] = swap(own, axis, bits)
    for bits in range(0, count, 4):
        blocks[bits ^ 2] = swap(blocks[bits], axis, 2)
    return [blocks[2 * at].reshape(-1, own.shape[-1]) for at in range(count // 2)]


def collide_kernel(chips, *refs):
    blocks, factors = refs[:chips], refs[chips : chips + 4]
    sent_ref, beside_ref = refs[chips + 4 :]
    me = lax.axis_index("mom")
    core, chip = me & 1, me >> 1
    rows, columns = blocks[0].shape[0], factors[0].shape[1]
    width = columns // RANK
    step = min(columns, 256)
    states = jnp.concatenate([block[...] for block in blocks], axis=0)
    total = jnp.zeros((chips * rows, 2 * width), jnp.float32)
    for which in range(2):
        a_ref, b_ref = factors[2 * which : 2 * which + 2]
        first = (core ^ which) * width
        for at in range(0, columns, step):
            proj_a = jnp.dot(states, a_ref[:, at : at + step], preferred_element_type=jnp.float32)
            proj_b = jnp.dot(states, b_ref[:, at : at + step], preferred_element_type=jnp.float32)
            product = proj_a * proj_b
            high = product.astype(jnp.bfloat16)
            low = (product - high.astype(jnp.float32)).astype(jnp.bfloat16)
            source = lax.broadcasted_iota(jnp.int32, (step, 2 * width), 0) + at
            target = lax.broadcasted_iota(jnp.int32, (step, 2 * width), 1)
            adds = jnp.where((source >> 3) + first == target, 1.0, 0.0).astype(jnp.bfloat16)
            total += jnp.dot(high, adds, preferred_element_type=jnp.float32)
            total += jnp.dot(low, adds, preferred_element_type=jnp.float32)
    terms = total.astype(jnp.bfloat16)
    away = 2 * core - 1
    for at in range(chips):
        here = chip ^ at
        part = terms[at * rows : (at + 1) * rows]
        sent_ref[here, 0] = part
        sent_ref[(here + away) & (chips - 1), 1] = part

        @pl.when(here == ((chip - away) & (chips - 1)))
        def _():
            beside_ref[...] = blocks[at][...]


def collide(blocks, factors):
    chips, (rows, size) = len(blocks), blocks[0].shape
    columns = factors[0].shape[1]
    whole = pl.BlockSpec(memory_space=pltpu.VMEM)
    return pl.pallas_call(
        functools.partial(collide_kernel, chips),
        out_shape=(
            jax.ShapeDtypeStruct((chips, 2, rows, 2 * columns // RANK), jnp.bfloat16),
            jax.ShapeDtypeStruct((rows, size), jnp.bfloat16),
        ),
        in_specs=[whole] * (chips + 4),
        out_specs=(whole, whole),
        compiler_params=pltpu.CompilerParams(vmem_limit_bytes=16 << 20),
        cost_estimate=pl.CostEstimate(
            flops=8 * chips * rows * size * columns,
            bytes_accessed=2 * (chips * rows * size + 4 * size * columns),
            transcendentals=0,
        ),
    )(*blocks, *factors)


def x_halo(cells, axis, dtype):
    count = lax.axis_size(axis)
    size = cells.shape[0]
    head = cells[:1].astype(dtype)
    tail = cells[size - 1 :].astype(dtype)
    if count == 2:
        both = swap(jnp.concatenate([tail, head], axis=0), axis, 1)
        behind, ahead = both[:1], both[1:]
    else:
        behind = lax.ppermute(tail, axis, [(i, (i + 1) % count) for i in range(count)])
        ahead = lax.ppermute(head, axis, [((i + 1) % count, i) for i in range(count)])
    return behind.astype(cells.dtype), ahead.astype(cells.dtype)


def upwind(center, behind, beyond, speeds):
    return jnp.maximum(speeds, 0.0) * (center - behind) + jnp.minimum(speeds, 0.0) * (
        beyond - center
    )


def per_device(distribution, a_factor, b_factor, velocity, drift):
    layers, owned, depth, size = distribution.shape
    assert owned == 1
    chips = lax.axis_size("mom") // 2
    odd = lax.axis_index("mom") % 2 == 1
    same = [[c + 2 * k for k in range(chips)] for c in range(2)]
    factors = (a_factor, b_factor, swap(a_factor, "mom", 1), swap(b_factor, "mom", 1))
    state = distribution.reshape(layers, depth, size)
    for substep in range(ITERS):
        sent, beside = collide(gathered(state.astype(jnp.bfloat16), "mom"), factors)
        got = lax.all_to_all(
            sent, "mom", split_axis=0, concat_axis=0, tiled=True, axis_index_groups=same
        )
        got = jnp.moveaxis(got, 0, 2).reshape(2, layers, depth, size).astype(jnp.float32)
        collided = state + collide_rate * got[0]
        beside = beside.astype(jnp.float32).reshape(state.shape) + collide_rate * got[1]
        x_behind, x_ahead = x_halo(collided, "space", jnp.bfloat16)
        near, far = swap(jnp.stack([collided, beside]).astype(jnp.bfloat16), "mom", 1).astype(
            jnp.float32
        )
        y_behind = jnp.where(odd, near, far)
        y_ahead = jnp.where(odd, far, near)
        x_behind = jnp.concatenate([x_behind, collided[:-1]], axis=0)
        x_ahead = jnp.concatenate([collided[1:], x_ahead], axis=0)
        read = collided - courant * upwind(collided, x_behind, x_ahead, velocity[0])
        read = read - courant * upwind(collided, y_behind, y_ahead, velocity[1])
        read = read - courant * upwind(
            collided, jnp.roll(collided, 1, axis=1), jnp.roll(collided, -1, axis=1), velocity[2]
        )
        upper = jnp.concatenate(
            [read[..., NDIR:], jnp.zeros(read.shape[:2] + (NDIR,), jnp.float32)], axis=2
        )
        state = read + drift * (upper - read)
    return state.reshape(distribution.shape)


def solution(mesh):
    in_specs = (P("space", "mom", None, None), P(None, "mom"), P(None, "mom"), P(), P())
    out_specs = P("space", "mom", None, None)
    return jax.shard_map(
        per_device, mesh=mesh, in_specs=in_specs, out_specs=out_specs, check_vma=False
    )
```

```python
import functools

import jax
import jax.numpy as jnp
from jax import lax
from jax.experimental import pallas as pl
from jax.experimental.pallas import tpu as pltpu
from jax.sharding import PartitionSpec as P

P_SIZE = 1024
RANK = 8
NDIR = 16
ITERS = 2


collide_rate = 0.1
courant = 0.3


def swap(block, axis, bits):
    count = lax.axis_size(axis)
    return lax.ppermute(block, axis, [(i, i ^ bits) for i in range(count)])


def gathered(own, axis):
    count = lax.axis_size(axis)
    blocks = {0: own}
    for bits in range(4, count, 4):
        blocks[bits] = swap(own, axis, bits)
    for bits in range(0, count, 4):
        blocks[bits ^ 2] = swap(blocks[bits], axis, 2)
    return [blocks[2 * at].reshape(-1, own.shape[-1]) for at in range(count // 2)]


def off_chip(array):
    return pltpu.with_memory_space_constraint(array, pltpu.MemorySpace.HBM)


def prepare_kernel(
    state_hbm, velocity_hbm, drift_hbm, state_ref, rounded_ref, tables_ref, velocity_ref, drift_ref, sems
):
    copies = [
        pltpu.make_async_copy(source, target, sems.at[at])
        for at, (source, target) in enumerate(
            ((state_hbm, state_ref), (velocity_hbm, velocity_ref), (drift_hbm, drift_ref))
        )
    ]
    for copy in copies:
        copy.start()
    for copy in copies:
        copy.wait()
    rounded_ref[...] = state_ref[...].astype(jnp.bfloat16)
    for dim in range(3):
        speeds = velocity_ref[dim : dim + 1, :]
        tables_ref[2 * dim : 2 * dim + 1, :] = jnp.maximum(speeds, 0.0)
        tables_ref[2 * dim + 1 : 2 * dim + 2, :] = jnp.minimum(speeds, 0.0)
    tables_ref[6:7, :] = drift_ref[...]
    tables_ref[7:8, :] = drift_ref[...]


def prepare(state, velocity, drift):
    hbm = pl.BlockSpec(memory_space=pltpu.MemorySpace.HBM)
    whole = pl.BlockSpec(memory_space=pltpu.VMEM)
    return pl.pallas_call(
        prepare_kernel,
        out_shape=(
            jax.ShapeDtypeStruct(state.shape, jnp.float32),
            jax.ShapeDtypeStruct(state.shape, jnp.bfloat16),
            jax.ShapeDtypeStruct((8, state.shape[-1]), jnp.float32),
        ),
        in_specs=[hbm] * 3,
        out_specs=(whole,) * 3,
        scratch_shapes=[
            pltpu.VMEM(velocity.shape, jnp.float32),
            pltpu.VMEM((1, drift.shape[0]), jnp.float32),
            pltpu.SemaphoreType.DMA((3,)),
        ],
        compiler_params=pltpu.CompilerParams(vmem_limit_bytes=8 << 20),
        cost_estimate=pl.CostEstimate(
            flops=state.size, bytes_accessed=10 * state.size, transcendentals=0
        ),
    )(*[off_chip(each) for each in (state, velocity, drift.reshape(1, -1))])


def collide_kernel(chips, fetch, *refs):
    blocks, factors = refs[:chips], refs[chips : chips + 4]
    sent_ref, beside_ref = refs[chips + 4 : chips + 6]
    copies = []
    kept = factors[:2]
    if fetch:
        kept, sems = refs[chips + 6 : chips + 8], refs[chips + 8]
        part = kept[0].shape[0] // sems.shape[1]
        copies = [
            pltpu.make_async_copy(
                source.at[at * part : (at + 1) * part],
                target.at[at * part : (at + 1) * part],
                sems.at[which, at],
            )
            for which, (source, target) in enumerate(zip(factors[:2], kept))
            for at in range(sems.shape[1])
        ]
    for copy in copies:
        copy.start()
    me = lax.axis_index("mom")
    core, chip = me & 1, me >> 1
    rows, columns = blocks[0].shape[0], factors[0].shape[1]
    width = columns // RANK
    step = min(columns, 256)
    states = jnp.concatenate([block[...] for block in blocks], axis=0)
    total = jnp.zeros((chips * rows, 2 * width), jnp.float32)
    for other, (a_ref, b_ref) in ((1, factors[2:]), (0, kept)):
        if not other:
            for copy in copies:
                copy.wait()
        first = (core ^ other) * width
        for at in range(0, columns, step):
            proj_a = jnp.dot(states, a_ref[:, at : at + step], preferred_element_type=jnp.float32)
            proj_b = jnp.dot(states, b_ref[:, at : at + step], preferred_element_type=jnp.float32)
            product = proj_a * proj_b
            high = product.astype(jnp.bfloat16)
            low = (product - high.astype(jnp.float32)).astype(jnp.bfloat16)
            source = lax.broadcasted_iota(jnp.int32, (step, 2 * width), 0) + at
            target = lax.broadcasted_iota(jnp.int32, (step, 2 * width), 1)
            adds = jnp.where((source >> 3) + first == target, 1.0, 0.0).astype(jnp.bfloat16)
            total += jnp.dot(high, adds, preferred_element_type=jnp.float32)
            total += jnp.dot(low, adds, preferred_element_type=jnp.float32)
    terms = total.astype(jnp.bfloat16)
    away = 2 * core - 1
    for at in range(chips):
        here = chip ^ at
        part = terms[at * rows : (at + 1) * rows]
        sent_ref[here, 0] = part
        sent_ref[(here + away) & (chips - 1), 1] = part

        @pl.when(here == ((chip - away) & (chips - 1)))
        def _():
            beside_ref[...] = blocks[at][...]


def collide(blocks, factors, fetch):
    chips, (rows, size) = len(blocks), blocks[0].shape
    columns = factors[0].shape[1]
    whole = pl.BlockSpec(memory_space=pltpu.VMEM)
    hbm = pl.BlockSpec(memory_space=pltpu.MemorySpace.HBM)
    factor = pltpu.VMEM((size, columns), jnp.bfloat16)
    return pl.pallas_call(
        functools.partial(collide_kernel, chips, fetch),
        out_shape=[
            jax.ShapeDtypeStruct((chips, 2, rows, 2 * columns // RANK), jnp.bfloat16),
            jax.ShapeDtypeStruct((rows, size), jnp.bfloat16),
        ],
        in_specs=[whole] * chips + [hbm if fetch else whole] * 2 + [whole] * 2,
        out_specs=[whole] * 2,
        scratch_shapes=[factor, factor, pltpu.SemaphoreType.DMA((2, 4))] if fetch else [],
        compiler_params=pltpu.CompilerParams(vmem_limit_bytes=16 << 20),
        cost_estimate=pl.CostEstimate(
            flops=8 * chips * rows * size * columns,
            bytes_accessed=2 * (chips * rows * size + 4 * size * columns),
            transcendentals=0,
        ),
    )(*blocks, *[off_chip(each) if fetch else each for each in factors[:2]], *factors[2:])

def x_halo(cells, axis, dtype):
    count = lax.axis_size(axis)
    size = cells.shape[0]
    head = cells[:1].astype(dtype)
    tail = cells[size - 1 :].astype(dtype)
    if count == 2:
        both = swap(jnp.concatenate([tail, head], axis=0), axis, 1)
        behind, ahead = both[:1], both[1:]
    else:
        behind = lax.ppermute(tail, axis, [(i, (i + 1) % count) for i in range(count)])
        ahead = lax.ppermute(head, axis, [((i + 1) % count, i) for i in range(count)])
    return behind.astype(cells.dtype), ahead.astype(cells.dtype)


def upwind(center, behind, beyond, speeds):
    return speeds[0] * (center - behind) + speeds[1] * (beyond - center)


def per_device(distribution, a_factor, b_factor, velocity, drift):
    layers, owned, depth, size = distribution.shape
    assert owned == 1
    chips = lax.axis_size("mom") // 2
    odd = lax.axis_index("mom") % 2 == 1
    same = [[c + 2 * k for k in range(chips)] for c in range(2)]
    factors = (a_factor, b_factor, swap(a_factor, "mom", 1), swap(b_factor, "mom", 1))
    state, rounded, tables = prepare(distribution.reshape(layers, depth, size), velocity, drift)
    drift = tables[6]
    for substep in range(ITERS):
        sent, beside = collide(gathered(rounded, "mom"), factors, substep == 0)
        got = lax.all_to_all(
            sent, "mom", split_axis=0, concat_axis=0, tiled=True, axis_index_groups=same
        )
        got = jnp.moveaxis(got, 0, 2).reshape(2, layers, depth, size).astype(jnp.float32)
        collided = state + collide_rate * got[0]
        beside = beside.astype(jnp.float32).reshape(state.shape) + collide_rate * got[1]
        x_behind, x_ahead = x_halo(collided, "space", jnp.bfloat16)
        near, far = swap(jnp.stack([collided, beside]).astype(jnp.bfloat16), "mom", 1).astype(
            jnp.float32
        )
        y_behind = jnp.where(odd, near, far)
        y_ahead = jnp.where(odd, far, near)
        x_behind = jnp.concatenate([x_behind, collided[:-1]], axis=0)
        x_ahead = jnp.concatenate([collided[1:], x_ahead], axis=0)
        read = collided - courant * upwind(collided, x_behind, x_ahead, tables[0:2])
        read = read - courant * upwind(collided, y_behind, y_ahead, tables[2:4])
        read = read - courant * upwind(
            collided, jnp.roll(collided, 1, axis=1), jnp.roll(collided, -1, axis=1), tables[4:6]
        )
        upper = jnp.concatenate(
            [read[..., NDIR:], jnp.zeros(read.shape[:2] + (NDIR,), jnp.float32)], axis=2
        )
        state = read + drift * (upper - read)
        rounded = state.astype(jnp.bfloat16)
    return state.reshape(distribution.shape)


def solution(mesh):
    in_specs = (P("space", "mom", None, None), P(None, "mom"), P(None, "mom"), P(), P())
    out_specs = P("space", "mom", None, None)
    return jax.shard_map(
        per_device, mesh=mesh, in_specs=in_specs, out_specs=out_specs, check_vma=False
    )
```

```python
import functools

import jax
import jax.numpy as jnp
from jax import lax
from jax.experimental import pallas as pl
from jax.experimental.pallas import tpu as pltpu
from jax.sharding import PartitionSpec as P

P_SIZE = 1024
RANK = 8
NDIR = 16
ITERS = 2


collide_rate = 0.1
courant = 0.3


def swap(block, axis, bits):
    count = lax.axis_size(axis)
    return lax.ppermute(block, axis, [(i, i ^ bits) for i in range(count)])


def gathered(own, axis):
    count = lax.axis_size(axis)
    blocks = {0: own}
    for bits in range(4, count, 4):
        blocks[bits] = swap(own, axis, bits)
    for bits in range(0, count, 4):
        blocks[bits ^ 2] = swap(blocks[bits], axis, 2)
    return [blocks[2 * at] for at in range(count // 2)]


def off_chip(array):
    return pltpu.with_memory_space_constraint(array, pltpu.MemorySpace.HBM)


def prepare_kernel(
    state_hbm, velocity_hbm, drift_hbm, state_ref, rounded_ref, tables_ref, velocity_ref, drift_ref, sems
):
    copies = [
        pltpu.make_async_copy(source, target, sems.at[at])
        for at, (source, target) in enumerate(
            ((state_hbm, state_ref), (velocity_hbm, velocity_ref), (drift_hbm, drift_ref))
        )
    ]
    for copy in copies:
        copy.start()
    for copy in copies:
        copy.wait()
    rounded_ref[...] = state_ref[...].astype(jnp.bfloat16)
    for dim in range(3):
        speeds = velocity_ref[dim : dim + 1, :]
        tables_ref[2 * dim : 2 * dim + 1, :] = jnp.maximum(speeds, 0.0)
        tables_ref[2 * dim + 1 : 2 * dim + 2, :] = jnp.minimum(speeds, 0.0)
    tables_ref[6:7, :] = drift_ref[...]
    tables_ref[7:8, :] = drift_ref[...]


def prepare(state, velocity, drift):
    hbm = pl.BlockSpec(memory_space=pltpu.MemorySpace.HBM)
    whole = pl.BlockSpec(memory_space=pltpu.VMEM)
    return pl.pallas_call(
        prepare_kernel,
        out_shape=(
            jax.ShapeDtypeStruct(state.shape, jnp.float32),
            jax.ShapeDtypeStruct(state.shape, jnp.bfloat16),
            jax.ShapeDtypeStruct((8, state.shape[-1]), jnp.float32),
        ),
        in_specs=[hbm] * 3,
        out_specs=(whole,) * 3,
        scratch_shapes=[
            pltpu.VMEM(velocity.shape, jnp.float32),
            pltpu.VMEM((1, drift.shape[0]), jnp.float32),
            pltpu.SemaphoreType.DMA((3,)),
        ],
        compiler_params=pltpu.CompilerParams(vmem_limit_bytes=8 << 20),
        cost_estimate=pl.CostEstimate(
            flops=state.size, bytes_accessed=10 * state.size, transcendentals=0
        ),
    )(*[off_chip(each) for each in (state, velocity, drift.reshape(1, -1))])


def project(states, core, partner, own, copies):
    columns = partner[0].shape[1]
    width = columns // RANK
    step = min(columns, 256)
    total = jnp.zeros((states.shape[0], 2 * width), jnp.float32)
    for other, (a_ref, b_ref) in ((1, partner), (0, own)):
        if not other:
            for copy in copies:
                copy.wait()
        first = (core ^ other) * width
        for at in range(0, columns, step):
            proj_a = jnp.dot(states, a_ref[:, at : at + step], preferred_element_type=jnp.float32)
            proj_b = jnp.dot(states, b_ref[:, at : at + step], preferred_element_type=jnp.float32)
            product = proj_a * proj_b
            high = product.astype(jnp.bfloat16)
            low = (product - high.astype(jnp.float32)).astype(jnp.bfloat16)
            source = lax.broadcasted_iota(jnp.int32, (step, 2 * width), 0) + at
            target = lax.broadcasted_iota(jnp.int32, (step, 2 * width), 1)
            adds = jnp.where((source >> 3) + first == target, 1.0, 0.0).astype(jnp.bfloat16)
            total += jnp.dot(high, adds, preferred_element_type=jnp.float32)
            total += jnp.dot(low, adds, preferred_element_type=jnp.float32)
    return total


def fetches(factors, kept, sems):
    part = kept[0].shape[0] // sems.shape[1]
    copies = [
        pltpu.make_async_copy(
            source.at[at * part : (at + 1) * part],
            target.at[at * part : (at + 1) * part],
            sems.at[which, at],
        )
        for which, (source, target) in enumerate(zip(factors, kept))
        for at in range(sems.shape[1])
    ]
    for copy in copies:
        copy.start()
    return copies


def collide_kernel(chips, fetch, *refs):
    blocks, factors = refs[:chips], refs[chips : chips + 4]
    sent_ref, beside_ref = refs[chips + 4 : chips + 6]
    copies, kept = [], factors[:2]
    if fetch:
        kept = refs[chips + 6 : chips + 8]
        copies = fetches(factors[:2], kept, refs[chips + 8])
    me = lax.axis_index("mom")
    core, chip = me & 1, me >> 1
    rows = blocks[0].shape[0]
    states = jnp.concatenate([block[...] for block in blocks], axis=0)
    total = project(states, core, factors[2:], kept, copies)
    terms = total.astype(jnp.bfloat16)
    away = 2 * core - 1
    for at in range(chips):
        here = chip ^ at
        part = terms[at * rows : (at + 1) * rows]
        sent_ref[here, 0] = part
        sent_ref[(here + away) & (chips - 1), 1] = part

        @pl.when(here == ((chip - away) & (chips - 1)))
        def _():
            beside_ref[...] = blocks[at][...]


def collide(blocks, factors, fetch):
    chips, (rows, size) = len(blocks), blocks[0].shape
    columns = factors[0].shape[1]
    whole = pl.BlockSpec(memory_space=pltpu.VMEM)
    hbm = pl.BlockSpec(memory_space=pltpu.MemorySpace.HBM)
    factor = pltpu.VMEM((size, columns), jnp.bfloat16)
    return pl.pallas_call(
        functools.partial(collide_kernel, chips, fetch),
        out_shape=[
            jax.ShapeDtypeStruct((chips, 2, rows, 2 * columns // RANK), jnp.bfloat16),
            jax.ShapeDtypeStruct((rows, size), jnp.bfloat16),
        ],
        in_specs=[whole] * chips + [hbm if fetch else whole] * 2 + [whole] * 2,
        out_specs=[whole] * 2,
        scratch_shapes=[factor, factor, pltpu.SemaphoreType.DMA((2, 4))] if fetch else [],
        compiler_params=pltpu.CompilerParams(vmem_limit_bytes=16 << 20),
        cost_estimate=pl.CostEstimate(
            flops=8 * chips * rows * size * columns,
            bytes_accessed=2 * (chips * rows * size + 4 * size * columns),
            transcendentals=0,
        ),
    )(*blocks, *[off_chip(each) if fetch else each for each in factors[:2]], *factors[2:])

def first_kernel(chips, layers, *refs):
    blocks, factors = refs[:chips], refs[chips : chips + 4]
    terms_ref, edges_ref, a_kept, b_kept, sems = refs[chips + 4 :]
    kept = (a_kept, b_kept)
    copies = fetches(factors[:2], kept, sems)
    me = lax.axis_index("mom")
    core, chip = me & 1, me >> 1
    rows = blocks[0].shape[0]
    depth = rows // layers
    states = jnp.concatenate([block[...] for block in blocks], axis=0)
    total = project(states, core, factors[2:], kept, copies)
    mine = total.shape[1]
    columns = pl.ds(pl.multiple_of(chip * mine, 128), mine)
    for at in range(chips):
        here = chip ^ at
        terms = total[at * rows : (at + 1) * rows].astype(jnp.bfloat16)
        terms_ref[here] = terms
        collided = blocks[at][:, columns].astype(jnp.float32)
        collided += collide_rate * terms.astype(jnp.float32)
        edges = jnp.concatenate([collided[rows - depth :], collided[:depth]], axis=0)
        edges_ref[here] = edges.astype(jnp.bfloat16)


def first_collision(blocks, factors, layers):
    chips, (rows, size) = len(blocks), blocks[0].shape
    columns = factors[0].shape[1]
    mine = 2 * columns // RANK
    whole = pl.BlockSpec(memory_space=pltpu.VMEM)
    hbm = pl.BlockSpec(memory_space=pltpu.MemorySpace.HBM)
    factor = pltpu.VMEM((size, columns), jnp.bfloat16)
    return pl.pallas_call(
        functools.partial(first_kernel, chips, layers),
        out_shape=[
            jax.ShapeDtypeStruct((chips, rows, mine), jnp.bfloat16),
            jax.ShapeDtypeStruct((chips, 2 * rows // layers, mine), jnp.bfloat16),
        ],
        in_specs=[whole] * chips + [hbm] * 2 + [whole] * 2,
        out_specs=[whole] * 2,
        scratch_shapes=[factor, factor, pltpu.SemaphoreType.DMA((2, 4))],
        compiler_params=pltpu.CompilerParams(vmem_limit_bytes=16 << 20),
        cost_estimate=pl.CostEstimate(
            flops=8 * chips * rows * size * columns,
            bytes_accessed=2 * (chips * rows * size + 4 * size * columns),
            transcendentals=0,
        ),
    )(*blocks, *[off_chip(each) for each in factors[:2]], *factors[2:])


def collided_kernel(chips, rows, state_ref, *refs):
    blocks, parts = refs[:chips], refs[chips : 2 * chips]
    exact_ref, edges_ref, rounded_ref = refs[2 * chips :]
    chip = lax.axis_index("mom") >> 1
    mine = parts[0].shape[2]
    for source in range(chips):
        columns = pl.ds(pl.multiple_of((chip ^ source) * mine, 128), mine)
        for at in range(chips):
            here = chip ^ at
            part = parts[source][here].astype(jnp.float32)
            if at:
                state = blocks[at][:, columns].astype(jnp.float32)
            else:
                state = state_ref[:, columns]
            collided = state + collide_rate * part[:rows]
            exact_ref[here, :, columns] = collided
            rounded_ref[here, :, columns] = collided.astype(jnp.bfloat16)
            edges_ref[here, :, columns] = part[rows:]


def collided_cells(state, blocks, parts):
    chips, (rows, size) = len(blocks), blocks[0].shape
    edge = parts[0].shape[1] - rows
    return pl.pallas_call(
        functools.partial(collided_kernel, chips, rows),
        out_shape=[
            jax.ShapeDtypeStruct((chips, rows, size), jnp.float32),
            jax.ShapeDtypeStruct((chips, edge, size), jnp.float32),
            jax.ShapeDtypeStruct((chips, rows, size), jnp.bfloat16),
        ],
        compiler_params=pltpu.CompilerParams(vmem_limit_bytes=16 << 20),
        cost_estimate=pl.CostEstimate(
            flops=2 * chips * rows * size, bytes_accessed=10 * chips * rows * size, transcendentals=0
        ),
    )(state, *blocks, *parts)


def second_kernel(chips, layers, exact_ref, edges_ref, other_ref, tables_ref, *refs):
    factors = refs[:4]
    sent_ref, own_ref, beside_ref, read_ref, states_ref = refs[4:]
    me = lax.axis_index("mom")
    core, chip = me & 1, me >> 1
    away = 2 * core - 1
    _, rows, size = exact_ref.shape
    depth = rows // layers
    read_ref[:, size:] = jnp.zeros((rows, read_ref.shape[1] - size), jnp.float32)

    @pl.loop(0, chips)
    def _(cell):
        before, after = (cell - 1 + core) & (chips - 1), (cell + core) & (chips - 1)
        for at in range(0, size, 128):
            lanes = slice(at, at + 128)
            center = exact_ref[cell, :, lanes]
            edges = edges_ref[cell, :, lanes]
            behind = jnp.concatenate([edges[:depth], center[: rows - depth]], axis=0)
            ahead = jnp.concatenate([center[depth:], edges[depth:]], axis=0)
            read = center - courant * upwind(center, behind, ahead, tables_ref[0:2, lanes])
            behind = other_ref[before, :, lanes].astype(jnp.float32)
            ahead = other_ref[after, :, lanes].astype(jnp.float32)
            read = read - courant * upwind(center, behind, ahead, tables_ref[2:4, lanes])
            levels = center.reshape(layers, depth, 128)
            behind = pltpu.roll(levels, 1, 1).reshape(rows, 128)
            ahead = pltpu.roll(levels, depth - 1, 1).reshape(rows, 128)
            read = read - courant * upwind(center, behind, ahead, tables_ref[4:6, lanes])
            read_ref[:, lanes] = read
        for at in range(0, size, 128):
            lanes = slice(at, at + 128)
            read = read_ref[:, lanes]
            upper = read_ref[:, at + NDIR : at + NDIR + 128]
            state = read + tables_ref[6:7, lanes] * (upper - read)
            states_ref[cell, :, lanes] = state.astype(jnp.bfloat16)

            @pl.when(cell == chip)
            def _():
                own_ref[:, lanes] = state

            @pl.when(cell == ((chip - away) & (chips - 1)))
            def _():
                beside_ref[:, lanes] = state

    states = states_ref[...].reshape(chips * rows, size)
    terms = project(states, core, factors[2:], factors[:2], []).astype(jnp.bfloat16)
    for here in range(chips):
        part = terms[here * rows : (here + 1) * rows]
        sent_ref[here, 0] = part
        sent_ref[(here + away) & (chips - 1), 1] = part


def second_collision(exact, edges, other, tables, factors, layers):
    chips, rows, size = exact.shape
    columns = factors[0].shape[1]
    return pl.pallas_call(
        functools.partial(second_kernel, chips, layers),
        out_shape=[
            jax.ShapeDtypeStruct((chips, 2, rows, 2 * columns // RANK), jnp.bfloat16),
            jax.ShapeDtypeStruct((rows, size), jnp.float32),
            jax.ShapeDtypeStruct((rows, size), jnp.float32),
        ],
        scratch_shapes=[
            pltpu.VMEM((rows, size + 128), jnp.float32),
            pltpu.VMEM((chips, rows, size), jnp.bfloat16),
        ],
        compiler_params=pltpu.CompilerParams(vmem_limit_bytes=16 << 20),
        cost_estimate=pl.CostEstimate(
            flops=8 * chips * rows * size * columns,
            bytes_accessed=2 * (chips * rows * size + 4 * size * columns),
            transcendentals=0,
        ),
    )(exact, edges, other, tables, *factors)


def edge_layers(edges, axis):
    count = lax.axis_size(axis)
    if count == 2:
        return swap(edges, axis, 1)
    depth = edges.shape[1] // 2
    last, first = edges[:, :depth], edges[:, depth:]
    behind = lax.ppermute(last, axis, [(i, (i + 1) % count) for i in range(count)])
    ahead = lax.ppermute(first, axis, [((i + 1) % count, i) for i in range(count)])
    return jnp.concatenate([behind, ahead], axis=1)


def x_halo(cells, axis, dtype):
    count = lax.axis_size(axis)
    size = cells.shape[0]
    head = cells[:1].astype(dtype)
    tail = cells[size - 1 :].astype(dtype)
    if count == 2:
        both = swap(jnp.concatenate([tail, head], axis=0), axis, 1)
        behind, ahead = both[:1], both[1:]
    else:
        behind = lax.ppermute(tail, axis, [(i, (i + 1) % count) for i in range(count)])
        ahead = lax.ppermute(head, axis, [((i + 1) % count, i) for i in range(count)])
    return behind.astype(cells.dtype), ahead.astype(cells.dtype)


def upwind(center, behind, beyond, speeds):
    return speeds[0:1] * (center - behind) + speeds[1:2] * (beyond - center)


def per_device(distribution, a_factor, b_factor, velocity, drift):
    layers, owned, depth, size = distribution.shape
    assert owned == 1
    chips = lax.axis_size("mom") // 2
    factors = (a_factor, b_factor, swap(a_factor, "mom", 1), swap(b_factor, "mom", 1))
    state, rounded, tables = prepare(distribution.reshape(layers * depth, size), velocity, drift)
    if 2 * (a_factor.shape[1] // RANK) % 128:
        for substep in range(ITERS):
            sent, beside = collide(gathered(rounded, "mom"), factors, substep == 0)
            state = settle(state, sent, beside.astype(jnp.float32), tables, layers)
            rounded = state.astype(jnp.bfloat16)
        return state.reshape(distribution.shape)
    for substep in range(0, ITERS, 2):
        blocks = gathered(rounded, "mom")
        terms, edges = first_collision(blocks, factors, layers)
        parts = gathered(jnp.concatenate([terms, edge_layers(edges, "space")], axis=1), "mom")
        exact, edges, cells = collided_cells(state, blocks, parts)
        other = swap(cells, "mom", 1)
        sent, state, beside = second_collision(exact, edges, other, tables, factors, layers)
        state = settle(state, sent, beside, tables, layers)
        rounded = state.astype(jnp.bfloat16)
    return state.reshape(distribution.shape)


def settle(state, sent, beside, tables, layers):
    rows, size = state.shape
    shape = (layers, rows // layers, size)
    chips = sent.shape[0]
    odd = lax.axis_index("mom") % 2 == 1
    same = [[c + 2 * k for k in range(chips)] for c in range(2)]
    got = lax.all_to_all(
        sent, "mom", split_axis=0, concat_axis=0, tiled=True, axis_index_groups=same
    )
    got = jnp.moveaxis(got, 0, 2).reshape((2,) + shape).astype(jnp.float32)
    collided = state.reshape(shape) + collide_rate * got[0]
    beside = beside.reshape(shape) + collide_rate * got[1]
    x_behind, x_ahead = x_halo(collided, "space", jnp.bfloat16)
    near, far = swap(jnp.stack([collided, beside]).astype(jnp.bfloat16), "mom", 1).astype(
        jnp.float32
    )
    y_behind = jnp.where(odd, near, far)
    y_ahead = jnp.where(odd, far, near)
    x_behind = jnp.concatenate([x_behind, collided[:-1]], axis=0)
    x_ahead = jnp.concatenate([collided[1:], x_ahead], axis=0)
    read = collided - courant * upwind(collided, x_behind, x_ahead, tables[0:2])
    read = read - courant * upwind(collided, y_behind, y_ahead, tables[2:4])
    read = read - courant * upwind(
        collided, jnp.roll(collided, 1, axis=1), jnp.roll(collided, -1, axis=1), tables[4:6]
    )
    upper = jnp.concatenate(
        [read[..., NDIR:], jnp.zeros(read.shape[:2] + (NDIR,), jnp.float32)], axis=2
    )
    return (read + tables[6] * (upper - read)).reshape(rows, size)


def solution(mesh):
    in_specs = (P("space", "mom", None, None), P(None, "mom"), P(None, "mom"), P(), P())
    out_specs = P("space", "mom", None, None)
    return jax.shard_map(
        per_device, mesh=mesh, in_specs=in_specs, out_specs=out_specs, check_vma=False
    )
```

```python
import functools

import jax
import jax.numpy as jnp
from jax import lax
from jax.experimental import pallas as pl
from jax.experimental.pallas import tpu as pltpu
from jax.sharding import PartitionSpec as P

P_SIZE = 1024
RANK = 8
NDIR = 16
ITERS = 2


collide_rate = 0.1
courant = 0.3


def swap(block, axis, bits):
    count = lax.axis_size(axis)
    return lax.ppermute(block, axis, [(i, i ^ bits) for i in range(count)])


def gathered(own, axis):
    count = lax.axis_size(axis)
    blocks = {0: own}
    for bits in range(4, count, 4):
        blocks[bits] = swap(own, axis, bits)
    for bits in range(0, count, 4):
        blocks[bits ^ 2] = swap(blocks[bits], axis, 2)
    return [blocks[2 * at] for at in range(count // 2)]


def off_chip(array):
    return pltpu.with_memory_space_constraint(array, pltpu.MemorySpace.HBM)


def prepare_kernel(
    state_hbm, velocity_hbm, drift_hbm, state_ref, rounded_ref, tables_ref, velocity_ref, drift_ref, sems
):
    copies = [
        pltpu.make_async_copy(source, target, sems.at[at])
        for at, (source, target) in enumerate(
            ((state_hbm, state_ref), (velocity_hbm, velocity_ref), (drift_hbm, drift_ref))
        )
    ]
    for copy in copies:
        copy.start()
    for copy in copies:
        copy.wait()
    rounded_ref[...] = state_ref[...].astype(jnp.bfloat16)
    for dim in range(3):
        speeds = velocity_ref[dim : dim + 1, :]
        tables_ref[2 * dim : 2 * dim + 1, :] = jnp.maximum(speeds, 0.0)
        tables_ref[2 * dim + 1 : 2 * dim + 2, :] = jnp.minimum(speeds, 0.0)
    tables_ref[6:7, :] = drift_ref[...]
    tables_ref[7:8, :] = drift_ref[...]


def prepare(state, velocity, drift):
    hbm = pl.BlockSpec(memory_space=pltpu.MemorySpace.HBM)
    whole = pl.BlockSpec(memory_space=pltpu.VMEM)
    return pl.pallas_call(
        prepare_kernel,
        out_shape=(
            jax.ShapeDtypeStruct(state.shape, jnp.float32),
            jax.ShapeDtypeStruct(state.shape, jnp.bfloat16),
            jax.ShapeDtypeStruct((8, state.shape[-1]), jnp.float32),
        ),
        in_specs=[hbm] * 3,
        out_specs=(whole,) * 3,
        scratch_shapes=[
            pltpu.VMEM(velocity.shape, jnp.float32),
            pltpu.VMEM((1, drift.shape[0]), jnp.float32),
            pltpu.SemaphoreType.DMA((3,)),
        ],
        compiler_params=pltpu.CompilerParams(vmem_limit_bytes=8 << 20),
        cost_estimate=pl.CostEstimate(
            flops=state.size, bytes_accessed=10 * state.size, transcendentals=0
        ),
    )(*[off_chip(each) for each in (state, velocity, drift.reshape(1, -1))])


def project(states, core, partner, own, copies):
    columns = partner[0].shape[1]
    width = columns // RANK
    step = min(columns, 256)
    total = jnp.zeros((states.shape[0], 2 * width), jnp.float32)
    for other, (a_ref, b_ref) in ((1, partner), (0, own)):
        if not other:
            for copy in copies:
                copy.wait()
        first = (core ^ other) * width
        for at in range(0, columns, step):
            proj_a = jnp.dot(states, a_ref[:, at : at + step], preferred_element_type=jnp.float32)
            proj_b = jnp.dot(states, b_ref[:, at : at + step], preferred_element_type=jnp.float32)
            product = proj_a * proj_b
            high = product.astype(jnp.bfloat16)
            low = (product - high.astype(jnp.float32)).astype(jnp.bfloat16)
            source = lax.broadcasted_iota(jnp.int32, (step, 2 * width), 0) + at
            target = lax.broadcasted_iota(jnp.int32, (step, 2 * width), 1)
            adds = jnp.where((source >> 3) + first == target, 1.0, 0.0).astype(jnp.bfloat16)
            total += jnp.dot(high, adds, preferred_element_type=jnp.float32)
            total += jnp.dot(low, adds, preferred_element_type=jnp.float32)
    return total


def fetches(factors, kept, sems):
    part = kept[0].shape[0] // sems.shape[1]
    copies = [
        pltpu.make_async_copy(
            source.at[at * part : (at + 1) * part],
            target.at[at * part : (at + 1) * part],
            sems.at[which, at],
        )
        for which, (source, target) in enumerate(zip(factors, kept))
        for at in range(sems.shape[1])
    ]
    for copy in copies:
        copy.start()
    return copies


def collide_kernel(chips, fetch, *refs):
    blocks, factors = refs[:chips], refs[chips : chips + 4]
    sent_ref, beside_ref = refs[chips + 4 : chips + 6]
    copies, kept = [], factors[:2]
    if fetch:
        kept = refs[chips + 6 : chips + 8]
        copies = fetches(factors[:2], kept, refs[chips + 8])
    me = lax.axis_index("mom")
    core, chip = me & 1, me >> 1
    rows = blocks[0].shape[0]
    states = jnp.concatenate([block[...] for block in blocks], axis=0)
    total = project(states, core, factors[2:], kept, copies)
    terms = total.astype(jnp.bfloat16)
    away = 2 * core - 1
    for at in range(chips):
        here = chip ^ at
        part = terms[at * rows : (at + 1) * rows]
        sent_ref[here, 0] = part
        sent_ref[(here + away) & (chips - 1), 1] = part

        @pl.when(here == ((chip - away) & (chips - 1)))
        def _():
            beside_ref[...] = blocks[at][...]


def collide(blocks, factors, fetch):
    chips, (rows, size) = len(blocks), blocks[0].shape
    columns = factors[0].shape[1]
    whole = pl.BlockSpec(memory_space=pltpu.VMEM)
    hbm = pl.BlockSpec(memory_space=pltpu.MemorySpace.HBM)
    factor = pltpu.VMEM((size, columns), jnp.bfloat16)
    return pl.pallas_call(
        functools.partial(collide_kernel, chips, fetch),
        out_shape=[
            jax.ShapeDtypeStruct((chips, 2, rows, 2 * columns // RANK), jnp.bfloat16),
            jax.ShapeDtypeStruct((rows, size), jnp.bfloat16),
        ],
        in_specs=[whole] * chips + [hbm if fetch else whole] * 2 + [whole] * 2,
        out_specs=[whole] * 2,
        scratch_shapes=[factor, factor, pltpu.SemaphoreType.DMA((2, 4))] if fetch else [],
        compiler_params=pltpu.CompilerParams(vmem_limit_bytes=16 << 20),
        cost_estimate=pl.CostEstimate(
            flops=8 * chips * rows * size * columns,
            bytes_accessed=2 * (chips * rows * size + 4 * size * columns),
            transcendentals=0,
        ),
    )(*blocks, *[off_chip(each) if fetch else each for each in factors[:2]], *factors[2:])

def first_kernel(chips, layers, *refs):
    blocks, factors = refs[:chips], refs[chips : chips + 4]
    terms_ref, edges_ref, a_kept, b_kept, sems = refs[chips + 4 :]
    kept = (a_kept, b_kept)
    copies = fetches(factors[:2], kept, sems)
    me = lax.axis_index("mom")
    core, chip = me & 1, me >> 1
    rows = blocks[0].shape[0]
    depth = rows // layers
    states = jnp.concatenate([block[...] for block in blocks], axis=0)
    total = project(states, core, factors[2:], kept, copies)
    mine = total.shape[1]
    columns = pl.ds(pl.multiple_of(chip * mine, 128), mine)
    for at in range(chips):
        here = chip ^ at
        terms = total[at * rows : (at + 1) * rows].astype(jnp.bfloat16)
        terms_ref[here] = terms
        collided = blocks[at][:, columns].astype(jnp.float32)
        collided += collide_rate * terms.astype(jnp.float32)
        edges = jnp.concatenate([collided[rows - depth :], collided[:depth]], axis=0)
        edges_ref[here] = edges.astype(jnp.bfloat16)


def first_collision(blocks, factors, layers):
    chips, (rows, size) = len(blocks), blocks[0].shape
    columns = factors[0].shape[1]
    mine = 2 * columns // RANK
    whole = pl.BlockSpec(memory_space=pltpu.VMEM)
    hbm = pl.BlockSpec(memory_space=pltpu.MemorySpace.HBM)
    factor = pltpu.VMEM((size, columns), jnp.bfloat16)
    return pl.pallas_call(
        functools.partial(first_kernel, chips, layers),
        out_shape=[
            jax.ShapeDtypeStruct((chips, rows, mine), jnp.bfloat16),
            jax.ShapeDtypeStruct((chips, 2 * rows // layers, mine), jnp.bfloat16),
        ],
        in_specs=[whole] * chips + [hbm] * 2 + [whole] * 2,
        out_specs=[whole] * 2,
        scratch_shapes=[factor, factor, pltpu.SemaphoreType.DMA((2, 4))],
        compiler_params=pltpu.CompilerParams(vmem_limit_bytes=16 << 20),
        cost_estimate=pl.CostEstimate(
            flops=8 * chips * rows * size * columns,
            bytes_accessed=2 * (chips * rows * size + 4 * size * columns),
            transcendentals=0,
        ),
    )(*blocks, *[off_chip(each) for each in factors[:2]], *factors[2:])


def collided_kernel(chips, rows, state_ref, *refs):
    blocks, parts = refs[:chips], refs[chips : 2 * chips]
    exact_ref, edges_ref, rounded_ref = refs[2 * chips :]
    chip = lax.axis_index("mom") >> 1
    mine = parts[0].shape[2]
    for source in range(chips):
        columns = pl.ds(pl.multiple_of((chip ^ source) * mine, 128), mine)
        for at in range(chips):
            here = chip ^ at
            part = parts[source][here].astype(jnp.float32)
            if at:
                state = blocks[at][:, columns].astype(jnp.float32)
            else:
                state = state_ref[:, columns]
            collided = state + collide_rate * part[:rows]
            exact_ref[here, :, columns] = collided
            rounded_ref[here, :, columns] = collided.astype(jnp.bfloat16)
            edges_ref[here, :, columns] = part[rows:]


def collided_cells(state, blocks, parts):
    chips, (rows, size) = len(blocks), blocks[0].shape
    edge = parts[0].shape[1] - rows
    return pl.pallas_call(
        functools.partial(collided_kernel, chips, rows),
        out_shape=[
            jax.ShapeDtypeStruct((chips, rows, size), jnp.float32),
            jax.ShapeDtypeStruct((chips, edge, size), jnp.float32),
            jax.ShapeDtypeStruct((chips, rows, size), jnp.bfloat16),
        ],
        compiler_params=pltpu.CompilerParams(vmem_limit_bytes=16 << 20),
        cost_estimate=pl.CostEstimate(
            flops=2 * chips * rows * size, bytes_accessed=10 * chips * rows * size, transcendentals=0
        ),
    )(state, *blocks, *parts)


def second_kernel(chips, layers, exact_ref, edges_ref, other_ref, tables_ref, *refs):
    factors = refs[:4]
    sent_ref, own_ref, beside_ref, read_ref, states_ref, updated_ref = refs[4:]
    me = lax.axis_index("mom")
    core, chip = me & 1, me >> 1
    away = 2 * core - 1
    _, rows, size = exact_ref.shape
    depth = rows // layers
    read_ref[:, size:] = jnp.zeros((rows, read_ref.shape[1] - size), jnp.float32)

    @pl.loop(0, chips)
    def _(cell):
        before, after = (cell - 1 + core) & (chips - 1), (cell + core) & (chips - 1)
        for at in range(0, size, 128):
            lanes = slice(at, at + 128)
            center = exact_ref[cell, :, lanes]
            edges = edges_ref[cell, :, lanes]
            behind = jnp.concatenate([edges[:depth], center[: rows - depth]], axis=0)
            ahead = jnp.concatenate([center[depth:], edges[depth:]], axis=0)
            read = center - courant * upwind(center, behind, ahead, tables_ref[0:2, lanes])
            behind = other_ref[before, :, lanes].astype(jnp.float32)
            ahead = other_ref[after, :, lanes].astype(jnp.float32)
            read = read - courant * upwind(center, behind, ahead, tables_ref[2:4, lanes])
            levels = center.reshape(layers, depth, 128)
            behind = pltpu.roll(levels, 1, 1).reshape(rows, 128)
            ahead = pltpu.roll(levels, depth - 1, 1).reshape(rows, 128)
            read = read - courant * upwind(center, behind, ahead, tables_ref[4:6, lanes])
            read_ref[:, lanes] = read
        for at in range(0, size, 128):
            lanes = slice(at, at + 128)
            read = read_ref[:, lanes]
            upper = read_ref[:, at + NDIR : at + NDIR + 128]
            state = read + tables_ref[6:7, lanes] * (upper - read)
            states_ref[cell, :, lanes] = state.astype(jnp.bfloat16)
            updated_ref[cell, :, lanes] = state

    own_ref[...] = updated_ref[chip]
    beside_ref[...] = updated_ref[(chip - away) & (chips - 1)]
    states = states_ref[...].reshape(chips * rows, size)
    terms = project(states, core, factors[2:], factors[:2], []).astype(jnp.bfloat16)
    for here in range(chips):
        part = terms[here * rows : (here + 1) * rows]
        sent_ref[here, 0] = part
        sent_ref[(here + away) & (chips - 1), 1] = part


def second_collision(exact, edges, other, tables, factors, layers):
    chips, rows, size = exact.shape
    columns = factors[0].shape[1]
    return pl.pallas_call(
        functools.partial(second_kernel, chips, layers),
        out_shape=[
            jax.ShapeDtypeStruct((chips, 2, rows, 2 * columns // RANK), jnp.bfloat16),
            jax.ShapeDtypeStruct((rows, size), jnp.float32),
            jax.ShapeDtypeStruct((rows, size), jnp.float32),
        ],
        scratch_shapes=[
            pltpu.VMEM((rows, size + 128), jnp.float32),
            pltpu.VMEM((chips, rows, size), jnp.bfloat16),
            pltpu.VMEM((chips, rows, size), jnp.float32),
        ],
        compiler_params=pltpu.CompilerParams(vmem_limit_bytes=16 << 20),
        cost_estimate=pl.CostEstimate(
            flops=8 * chips * rows * size * columns,
            bytes_accessed=2 * (chips * rows * size + 4 * size * columns),
            transcendentals=0,
        ),
    )(exact, edges, other, tables, *factors)


def edge_layers(edges, axis):
    count = lax.axis_size(axis)
    if count == 2:
        return swap(edges, axis, 1)
    depth = edges.shape[1] // 2
    last, first = edges[:, :depth], edges[:, depth:]
    behind = lax.ppermute(last, axis, [(i, (i + 1) % count) for i in range(count)])
    ahead = lax.ppermute(first, axis, [((i + 1) % count, i) for i in range(count)])
    return jnp.concatenate([behind, ahead], axis=1)


def x_halo(cells, axis, dtype):
    count = lax.axis_size(axis)
    size = cells.shape[0]
    head = cells[:1].astype(dtype)
    tail = cells[size - 1 :].astype(dtype)
    if count == 2:
        both = swap(jnp.concatenate([tail, head], axis=0), axis, 1)
        behind, ahead = both[:1], both[1:]
    else:
        behind = lax.ppermute(tail, axis, [(i, (i + 1) % count) for i in range(count)])
        ahead = lax.ppermute(head, axis, [((i + 1) % count, i) for i in range(count)])
    return behind.astype(cells.dtype), ahead.astype(cells.dtype)


def upwind(center, behind, beyond, speeds):
    return speeds[0:1] * (center - behind) + speeds[1:2] * (beyond - center)


def per_device(distribution, a_factor, b_factor, velocity, drift):
    layers, owned, depth, size = distribution.shape
    assert owned == 1
    chips = lax.axis_size("mom") // 2
    factors = (a_factor, b_factor, swap(a_factor, "mom", 1), swap(b_factor, "mom", 1))
    state, rounded, tables = prepare(distribution.reshape(layers * depth, size), velocity, drift)
    if 2 * (a_factor.shape[1] // RANK) % 128:
        for substep in range(ITERS):
            sent, beside = collide(gathered(rounded, "mom"), factors, substep == 0)
            state = settle(state, sent, beside.astype(jnp.float32), tables, layers)
            rounded = state.astype(jnp.bfloat16)
        return state.reshape(distribution.shape)
    for substep in range(0, ITERS, 2):
        blocks = gathered(rounded, "mom")
        terms, edges = first_collision(blocks, factors, layers)
        parts = gathered(jnp.concatenate([terms, edge_layers(edges, "space")], axis=1), "mom")
        exact, edges, cells = collided_cells(state, blocks, parts)
        other = swap(cells, "mom", 1)
        sent, state, beside = second_collision(exact, edges, other, tables, factors, layers)
        state = settle(state, sent, beside, tables, layers)
        rounded = state.astype(jnp.bfloat16)
    return state.reshape(distribution.shape)


def settle(state, sent, beside, tables, layers):
    rows, size = state.shape
    shape = (layers, rows // layers, size)
    chips = sent.shape[0]
    odd = lax.axis_index("mom") % 2 == 1
    same = [[c + 2 * k for k in range(chips)] for c in range(2)]
    got = lax.all_to_all(
        sent, "mom", split_axis=0, concat_axis=0, tiled=True, axis_index_groups=same
    )
    got = jnp.moveaxis(got, 0, 2).reshape((2,) + shape).astype(jnp.float32)
    collided = state.reshape(shape) + collide_rate * got[0]
    beside = beside.reshape(shape) + collide_rate * got[1]
    x_behind, x_ahead = x_halo(collided, "space", jnp.bfloat16)
    near, far = swap(jnp.stack([collided, beside]).astype(jnp.bfloat16), "mom", 1).astype(
        jnp.float32
    )
    y_behind = jnp.where(odd, near, far)
    y_ahead = jnp.where(odd, far, near)
    x_behind = jnp.concatenate([x_behind, collided[:-1]], axis=0)
    x_ahead = jnp.concatenate([collided[1:], x_ahead], axis=0)
    read = collided - courant * upwind(collided, x_behind, x_ahead, tables[0:2])
    read = read - courant * upwind(collided, y_behind, y_ahead, tables[2:4])
    read = read - courant * upwind(
        collided, jnp.roll(collided, 1, axis=1), jnp.roll(collided, -1, axis=1), tables[4:6]
    )
    upper = jnp.concatenate(
        [read[..., NDIR:], jnp.zeros(read.shape[:2] + (NDIR,), jnp.float32)], axis=2
    )
    return (read + tables[6] * (upper - read)).reshape(rows, size)


def solution(mesh):
    in_specs = (P("space", "mom", None, None), P(None, "mom"), P(None, "mom"), P(), P())
    out_specs = P("space", "mom", None, None)
    return jax.shard_map(
        per_device, mesh=mesh, in_specs=in_specs, out_specs=out_specs, check_vma=False
    )
```

```python
import functools

import jax
import jax.numpy as jnp
from jax import lax
from jax.experimental import pallas as pl
from jax.experimental.pallas import tpu as pltpu
from jax.sharding import PartitionSpec as P


RANK = 8
NDIR = 16
ITERS = 2


collide_rate = 0.1
courant = 0.3


def swap(block, axis, bits):
    count = lax.axis_size(axis)
    return lax.ppermute(block, axis, [(i, i ^ bits) for i in range(count)])


def gathered(own, axis):
    count = lax.axis_size(axis)
    blocks = {0: own}
    for bits in range(4, count, 4):
        blocks[bits] = swap(own, axis, bits)
    for bits in range(0, count, 4):
        blocks[bits ^ 2] = swap(blocks[bits], axis, 2)
    return [blocks[2 * at] for at in range(count // 2)]


def off_chip(array):
    return pltpu.with_memory_space_constraint(array, pltpu.MemorySpace.HBM)


def prepare_kernel(
    state_hbm, velocity_hbm, drift_hbm, state_ref, rounded_ref, tables_ref, velocity_ref, drift_ref, sems
):
    copies = [
        pltpu.make_async_copy(source, target, sems.at[at])
        for at, (source, target) in enumerate(
            ((state_hbm, state_ref), (velocity_hbm, velocity_ref), (drift_hbm, drift_ref))
        )
    ]
    for copy in copies:
        copy.start()
    for copy in copies:
        copy.wait()
    rounded_ref[...] = state_ref[...].astype(jnp.bfloat16)
    for dim in range(3):
        speeds = velocity_ref[dim : dim + 1, :]
        tables_ref[2 * dim : 2 * dim + 1, :] = jnp.maximum(speeds, 0.0)
        tables_ref[2 * dim + 1 : 2 * dim + 2, :] = jnp.minimum(speeds, 0.0)
    tables_ref[6:7, :] = drift_ref[...]
    tables_ref[7:8, :] = drift_ref[...]


def prepare(state, velocity, drift):
    hbm = pl.BlockSpec(memory_space=pltpu.MemorySpace.HBM)
    whole = pl.BlockSpec(memory_space=pltpu.VMEM)
    return pl.pallas_call(
        prepare_kernel,
        out_shape=(
            jax.ShapeDtypeStruct(state.shape, jnp.float32),
            jax.ShapeDtypeStruct(state.shape, jnp.bfloat16),
            jax.ShapeDtypeStruct((8, state.shape[-1]), jnp.float32),
        ),
        in_specs=[hbm] * 3,
        out_specs=(whole,) * 3,
        scratch_shapes=[
            pltpu.VMEM(velocity.shape, jnp.float32),
            pltpu.VMEM((1, drift.shape[0]), jnp.float32),
            pltpu.SemaphoreType.DMA((3,)),
        ],
        compiler_params=pltpu.CompilerParams(vmem_limit_bytes=8 << 20),
        cost_estimate=pl.CostEstimate(
            flops=state.size, bytes_accessed=10 * state.size, transcendentals=0
        ),
    )(*[off_chip(each) for each in (state, velocity, drift.reshape(1, -1))])


def project(states, core, partner, own, copies):
    columns = partner[0].shape[1]
    width = columns // RANK
    step = min(columns, 256)
    total = jnp.zeros((states.shape[0], 2 * width), jnp.float32)
    for other, (a_ref, b_ref) in ((1, partner), (0, own)):
        if not other:
            for copy in copies:
                copy.wait()
        first = (core ^ other) * width
        for at in range(0, columns, step):
            proj_a = jnp.dot(states, a_ref[:, at : at + step], preferred_element_type=jnp.float32)
            proj_b = jnp.dot(states, b_ref[:, at : at + step], preferred_element_type=jnp.float32)
            product = proj_a * proj_b
            high = product.astype(jnp.bfloat16)
            low = (product - high.astype(jnp.float32)).astype(jnp.bfloat16)
            source = lax.broadcasted_iota(jnp.int32, (step, 2 * width), 0) + at
            target = lax.broadcasted_iota(jnp.int32, (step, 2 * width), 1)
            adds = jnp.where((source >> 3) + first == target, 1.0, 0.0).astype(jnp.bfloat16)
            total += jnp.dot(high, adds, preferred_element_type=jnp.float32)
            total += jnp.dot(low, adds, preferred_element_type=jnp.float32)
    return total


def fetches(factors, kept, sems):
    part = kept[0].shape[0] // sems.shape[1]
    copies = [
        pltpu.make_async_copy(
            source.at[at * part : (at + 1) * part],
            target.at[at * part : (at + 1) * part],
            sems.at[which, at],
        )
        for which, (source, target) in enumerate(zip(factors, kept))
        for at in range(sems.shape[1])
    ]
    for copy in copies:
        copy.start()
    return copies


def collide_kernel(chips, fetch, *refs):
    blocks, factors = refs[:chips], refs[chips : chips + 4]
    sent_ref, beside_ref = refs[chips + 4 : chips + 6]
    copies, kept = [], factors[:2]
    if fetch:
        kept = refs[chips + 6 : chips + 8]
        copies = fetches(factors[:2], kept, refs[chips + 8])
    me = lax.axis_index("mom")
    core, chip = me & 1, me >> 1
    rows = blocks[0].shape[0]
    states = jnp.concatenate([block[...] for block in blocks], axis=0)
    total = project(states, core, factors[2:], kept, copies)
    terms = total.astype(jnp.bfloat16)
    away = 2 * core - 1
    for at in range(chips):
        here = chip ^ at
        part = terms[at * rows : (at + 1) * rows]
        sent_ref[here, 0] = part
        sent_ref[(here + away) & (chips - 1), 1] = part

        @pl.when(here == ((chip - away) & (chips - 1)))
        def _():
            beside_ref[...] = blocks[at][...]


def collide(blocks, factors, fetch):
    chips, (rows, size) = len(blocks), blocks[0].shape
    columns = factors[0].shape[1]
    whole = pl.BlockSpec(memory_space=pltpu.VMEM)
    hbm = pl.BlockSpec(memory_space=pltpu.MemorySpace.HBM)
    factor = pltpu.VMEM((size, columns), jnp.bfloat16)
    return pl.pallas_call(
        functools.partial(collide_kernel, chips, fetch),
        out_shape=[
            jax.ShapeDtypeStruct((chips, 2, rows, 2 * columns // RANK), jnp.bfloat16),
            jax.ShapeDtypeStruct((rows, size), jnp.bfloat16),
        ],
        in_specs=[whole] * chips + [hbm if fetch else whole] * 2 + [whole] * 2,
        out_specs=[whole] * 2,
        scratch_shapes=[factor, factor, pltpu.SemaphoreType.DMA((2, 4))] if fetch else [],
        compiler_params=pltpu.CompilerParams(vmem_limit_bytes=16 << 20),
        cost_estimate=pl.CostEstimate(
            flops=8 * chips * rows * size * columns,
            bytes_accessed=2 * (chips * rows * size + 4 * size * columns),
            transcendentals=0,
        ),
    )(*blocks, *[off_chip(each) if fetch else each for each in factors[:2]], *factors[2:])


def first_kernel(chips, layers, *refs):
    blocks, factors = refs[:chips], refs[chips : chips + 4]
    terms_ref, edges_ref, a_kept, b_kept, sems = refs[chips + 4 :]
    kept = (a_kept, b_kept)
    copies = fetches(factors[:2], kept, sems)
    me = lax.axis_index("mom")
    core, chip = me & 1, me >> 1
    rows = blocks[0].shape[0]
    depth = rows // layers
    states = jnp.concatenate([block[...] for block in blocks], axis=0)
    total = project(states, core, factors[2:], kept, copies)
    mine = total.shape[1]
    columns = pl.ds(pl.multiple_of(chip * mine, 128), mine)
    for at in range(chips):
        here = chip ^ at
        terms = total[at * rows : (at + 1) * rows].astype(jnp.bfloat16)
        terms_ref[here] = terms
        collided = blocks[at][:, columns].astype(jnp.float32)
        collided += collide_rate * terms.astype(jnp.float32)
        edges = jnp.concatenate([collided[rows - depth :], collided[:depth]], axis=0)
        edges_ref[here] = edges.astype(jnp.bfloat16)


def first_collision(blocks, factors, layers):
    chips, (rows, size) = len(blocks), blocks[0].shape
    columns = factors[0].shape[1]
    mine = 2 * columns // RANK
    whole = pl.BlockSpec(memory_space=pltpu.VMEM)
    hbm = pl.BlockSpec(memory_space=pltpu.MemorySpace.HBM)
    factor = pltpu.VMEM((size, columns), jnp.bfloat16)
    return pl.pallas_call(
        functools.partial(first_kernel, chips, layers),
        out_shape=[
            jax.ShapeDtypeStruct((chips, rows, mine), jnp.bfloat16),
            jax.ShapeDtypeStruct((chips, 2 * rows // layers, mine), jnp.bfloat16),
        ],
        in_specs=[whole] * chips + [hbm] * 2 + [whole] * 2,
        out_specs=[whole] * 2,
        scratch_shapes=[factor, factor, pltpu.SemaphoreType.DMA((2, 4))],
        compiler_params=pltpu.CompilerParams(vmem_limit_bytes=16 << 20),
        cost_estimate=pl.CostEstimate(
            flops=8 * chips * rows * size * columns,
            bytes_accessed=2 * (chips * rows * size + 4 * size * columns),
            transcendentals=0,
        ),
    )(*blocks, *[off_chip(each) for each in factors[:2]], *factors[2:])


def collided_kernel(chips, rows, state_ref, *refs):
    blocks, parts = refs[:chips], refs[chips : 2 * chips]
    exact_ref, edges_ref, rounded_ref = refs[2 * chips :]
    chip = lax.axis_index("mom") >> 1
    mine = parts[0].shape[2]
    for source in range(chips):
        columns = pl.ds(pl.multiple_of((chip ^ source) * mine, 128), mine)
        for at in range(chips):
            here = chip ^ at
            part = parts[source][here].astype(jnp.float32)
            if at:
                state = blocks[at][:, columns].astype(jnp.float32)
            else:
                state = state_ref[:, columns]
            collided = state + collide_rate * part[:rows]
            exact_ref[here, :, columns] = collided
            rounded_ref[here, :, columns] = collided.astype(jnp.bfloat16)
            edges_ref[here, :, columns] = part[rows:]


def collided_cells(state, blocks, parts):
    chips, (rows, size) = len(blocks), blocks[0].shape
    edge = parts[0].shape[1] - rows
    return pl.pallas_call(
        functools.partial(collided_kernel, chips, rows),
        out_shape=[
            jax.ShapeDtypeStruct((chips, rows, size), jnp.float32),
            jax.ShapeDtypeStruct((chips, edge, size), jnp.float32),
            jax.ShapeDtypeStruct((chips, rows, size), jnp.bfloat16),
        ],
        compiler_params=pltpu.CompilerParams(vmem_limit_bytes=16 << 20),
        cost_estimate=pl.CostEstimate(
            flops=2 * chips * rows * size, bytes_accessed=10 * chips * rows * size, transcendentals=0
        ),
    )(state, *blocks, *parts)


def inner_kernel(layers, exact_ref, edges_ref, tables_ref, read_ref):
    chips, rows, size = exact_ref.shape
    depth = rows // layers

    @pl.loop(0, chips)
    def _(cell):
        for at in range(0, size, 128):
            lanes = slice(at, at + 128)
            center = exact_ref[cell, :, lanes]
            edges = edges_ref[cell, :, lanes]
            behind = jnp.concatenate([edges[:depth], center[: rows - depth]], axis=0)
            ahead = jnp.concatenate([center[depth:], edges[depth:]], axis=0)
            read = center - courant * upwind(center, behind, ahead, tables_ref[0:2, lanes])
            levels = center.reshape(layers, depth, 128)
            behind = pltpu.roll(levels, 1, 1).reshape(rows, 128)
            ahead = pltpu.roll(levels, depth - 1, 1).reshape(rows, 128)
            read = read - courant * upwind(center, behind, ahead, tables_ref[4:6, lanes])
            speeds = tables_ref[2:3, lanes] - tables_ref[3:4, lanes]
            read_ref[cell, :, lanes] = read - courant * speeds * center


def inner_update(exact, edges, tables, layers):
    return pl.pallas_call(
        functools.partial(inner_kernel, layers),
        out_shape=jax.ShapeDtypeStruct(exact.shape, jnp.float32),
        compiler_params=pltpu.CompilerParams(vmem_limit_bytes=8 << 20),
        cost_estimate=pl.CostEstimate(
            flops=20 * exact.size, bytes_accessed=8 * exact.size, transcendentals=0
        ),
    )(exact, edges, tables)


def drifted(read, after, drift):
    rolled = pltpu.roll(read, 128 - NDIR, 1)
    inside = lax.broadcasted_iota(jnp.int32, read.shape, 1) < 128 - NDIR
    upper = jnp.where(inside, rolled, 0.0 if after is None else after)
    return read + drift * (upper - read), rolled


def second_kernel(chips, inner_ref, other_ref, tables_ref, *refs):
    factors = refs[:4]
    sent_ref, own_ref, beside_ref, states_ref, updated_ref = refs[4:]
    me = lax.axis_index("mom")
    core, chip = me & 1, me >> 1
    away = 2 * core - 1
    _, rows, size = inner_ref.shape

    @pl.loop(0, chips)
    def _(cell):
        before, after = (cell - 1 + core) & (chips - 1), (cell + core) & (chips - 1)
        rolled = None
        for at in reversed(range(0, size, 128)):
            lanes = slice(at, at + 128)
            speeds = courant * tables_ref[2:4, lanes]
            read = inner_ref[cell, :, lanes]
            read += speeds[0:1] * other_ref[before, :, lanes].astype(jnp.float32)
            read -= speeds[1:2] * other_ref[after, :, lanes].astype(jnp.float32)
            state, rolled = drifted(read, rolled, tables_ref[6:7, lanes])
            states_ref[cell, :, lanes] = state.astype(jnp.bfloat16)
            updated_ref[cell, :, lanes] = state

    own_ref[...] = updated_ref[chip]
    beside_ref[...] = updated_ref[(chip - away) & (chips - 1)]
    states = states_ref[...].reshape(chips * rows, size)
    terms = project(states, core, factors[2:], factors[:2], []).astype(jnp.bfloat16)
    for here in range(chips):
        part = terms[here * rows : (here + 1) * rows]
        sent_ref[here, 0] = part
        sent_ref[(here + away) & (chips - 1), 1] = part


def second_collision(inner, other, tables, factors):
    chips, rows, size = inner.shape
    columns = factors[0].shape[1]
    return pl.pallas_call(
        functools.partial(second_kernel, chips),
        out_shape=[
            jax.ShapeDtypeStruct((chips, 2, rows, 2 * columns // RANK), jnp.bfloat16),
            jax.ShapeDtypeStruct((rows, size), jnp.float32),
            jax.ShapeDtypeStruct((rows, size), jnp.float32),
        ],
        scratch_shapes=[
            pltpu.VMEM((chips, rows, size), jnp.bfloat16),
            pltpu.VMEM((chips, rows, size), jnp.float32),
        ],
        compiler_params=pltpu.CompilerParams(vmem_limit_bytes=16 << 20),
        cost_estimate=pl.CostEstimate(
            flops=8 * chips * rows * size * columns,
            bytes_accessed=2 * (chips * rows * size + 4 * size * columns),
            transcendentals=0,
        ),
    )(inner, other, tables, *factors)


def arrive_kernel(layers, got_ref, own_ref, beside_ref, exact_ref, edges_ref, cells_ref):
    chips, _, rows, mine = got_ref.shape
    depth = rows // layers
    for source in range(chips):
        lanes = slice(source * mine, (source + 1) * mine)
        collided = own_ref[:, lanes] + collide_rate * got_ref[source, 0].astype(jnp.float32)
        beyond = beside_ref[:, lanes] + collide_rate * got_ref[source, 1].astype(jnp.float32)
        exact_ref[:, lanes] = collided
        edges = jnp.concatenate([collided[rows - depth :], collided[:depth]], axis=0)
        edges_ref[0, :, lanes] = edges.astype(jnp.bfloat16)
        cells_ref[0, :, lanes] = collided.astype(jnp.bfloat16)
        cells_ref[1, :, lanes] = beyond.astype(jnp.bfloat16)


def last_kernel(layers, exact_ref, edges_ref, cells_ref, tables_ref, out_ref):
    core = lax.axis_index("mom") & 1
    rows, size = exact_ref.shape
    depth = rows // layers
    rolled = None
    for at in reversed(range(0, size, 128)):
        lanes = slice(at, at + 128)
        center = exact_ref[:, lanes]
        edges = edges_ref[0, :, lanes].astype(jnp.float32)
        behind = jnp.concatenate([edges[:depth], center[: rows - depth]], axis=0)
        ahead = jnp.concatenate([center[depth:], edges[depth:]], axis=0)
        read = center - courant * upwind(center, behind, ahead, tables_ref[0:2, lanes])
        behind = cells_ref[1 - core, :, lanes].astype(jnp.float32)
        ahead = cells_ref[core, :, lanes].astype(jnp.float32)
        read = read - courant * upwind(center, behind, ahead, tables_ref[2:4, lanes])
        levels = center.reshape(layers, depth, 128)
        behind = pltpu.roll(levels, 1, 1).reshape(rows, 128)
        ahead = pltpu.roll(levels, depth - 1, 1).reshape(rows, 128)
        read = read - courant * upwind(center, behind, ahead, tables_ref[4:6, lanes])
        out_ref[:, lanes], rolled = drifted(read, rolled, tables_ref[6:7, lanes])


def settled(state, sent, beside, tables, layers):
    rows, size = state.shape
    chips = sent.shape[0]
    same = [[c + 2 * k for k in range(chips)] for c in range(2)]
    got = lax.all_to_all(
        sent, "mom", split_axis=0, concat_axis=0, tiled=True, axis_index_groups=same
    )
    params = pltpu.CompilerParams(vmem_limit_bytes=4 << 20)
    cost = pl.CostEstimate(flops=20 * state.size, bytes_accessed=12 * state.size, transcendentals=0)
    exact, edges, cells = pl.pallas_call(
        functools.partial(arrive_kernel, layers),
        out_shape=[
            jax.ShapeDtypeStruct((rows, size), jnp.float32),
            jax.ShapeDtypeStruct((1, 2 * rows // layers, size), jnp.bfloat16),
            jax.ShapeDtypeStruct((2, rows, size), jnp.bfloat16),
        ],
        compiler_params=params,
        cost_estimate=cost,
    )(got, state, beside)
    edges = edge_layers(edges, "space")
    cells = swap(cells, "mom", 1)
    return pl.pallas_call(
        functools.partial(last_kernel, layers),
        out_shape=jax.ShapeDtypeStruct((rows, size), jnp.float32),
        compiler_params=params,
        cost_estimate=cost,
    )(exact, edges, cells, tables)


def edge_layers(edges, axis):
    count = lax.axis_size(axis)
    if count == 2:
        return swap(edges, axis, 1)
    depth = edges.shape[1] // 2
    last, first = edges[:, :depth], edges[:, depth:]
    behind = lax.ppermute(last, axis, [(i, (i + 1) % count) for i in range(count)])
    ahead = lax.ppermute(first, axis, [((i + 1) % count, i) for i in range(count)])
    return jnp.concatenate([behind, ahead], axis=1)


def x_halo(cells, axis, dtype):
    count = lax.axis_size(axis)
    size = cells.shape[0]
    head = cells[:1].astype(dtype)
    tail = cells[size - 1 :].astype(dtype)
    if count == 2:
        both = swap(jnp.concatenate([tail, head], axis=0), axis, 1)
        behind, ahead = both[:1], both[1:]
    else:
        behind = lax.ppermute(tail, axis, [(i, (i + 1) % count) for i in range(count)])
        ahead = lax.ppermute(head, axis, [((i + 1) % count, i) for i in range(count)])
    return behind.astype(cells.dtype), ahead.astype(cells.dtype)


def upwind(center, behind, beyond, speeds):
    return speeds[0:1] * (center - behind) + speeds[1:2] * (beyond - center)


def per_device(distribution, a_factor, b_factor, velocity, drift):
    layers, owned, depth, size = distribution.shape
    assert owned == 1
    factors = (a_factor, b_factor, swap(a_factor, "mom", 1), swap(b_factor, "mom", 1))
    state, rounded, tables = prepare(distribution.reshape(layers * depth, size), velocity, drift)
    if 2 * (a_factor.shape[1] // RANK) % 128:
        for substep in range(ITERS):
            sent, beside = collide(gathered(rounded, "mom"), factors, substep == 0)
            state = settle(state, sent, beside.astype(jnp.float32), tables, layers)
            rounded = state.astype(jnp.bfloat16)
        return state.reshape(distribution.shape)
    for _ in range(0, ITERS, 2):
        blocks = gathered(rounded, "mom")
        terms, edges = first_collision(blocks, factors, layers)
        parts = gathered(jnp.concatenate([terms, edge_layers(edges, "space")], axis=1), "mom")
        exact, edges, cells = collided_cells(state, blocks, parts)
        other = swap(cells, "mom", 1)
        inner = inner_update(exact, edges, tables, layers)
        sent, state, beside = second_collision(inner, other, tables, factors)
        state = settled(state, sent, beside, tables, layers)
        rounded = state.astype(jnp.bfloat16)
    return state.reshape(distribution.shape)


def settle(state, sent, beside, tables, layers):
    rows, size = state.shape
    shape = (layers, rows // layers, size)
    chips = sent.shape[0]
    odd = lax.axis_index("mom") % 2 == 1
    same = [[c + 2 * k for k in range(chips)] for c in range(2)]
    got = lax.all_to_all(
        sent, "mom", split_axis=0, concat_axis=0, tiled=True, axis_index_groups=same
    )
    got = jnp.moveaxis(got, 0, 2).reshape((2,) + shape).astype(jnp.float32)
    collided = state.reshape(shape) + collide_rate * got[0]
    beside = beside.reshape(shape) + collide_rate * got[1]
    x_behind, x_ahead = x_halo(collided, "space", jnp.bfloat16)
    near, far = swap(jnp.stack([collided, beside]).astype(jnp.bfloat16), "mom", 1).astype(
        jnp.float32
    )
    y_behind = jnp.where(odd, near, far)
    y_ahead = jnp.where(odd, far, near)
    x_behind = jnp.concatenate([x_behind, collided[:-1]], axis=0)
    x_ahead = jnp.concatenate([collided[1:], x_ahead], axis=0)
    read = collided - courant * upwind(collided, x_behind, x_ahead, tables[0:2])
    read = read - courant * upwind(collided, y_behind, y_ahead, tables[2:4])
    read = read - courant * upwind(
        collided, jnp.roll(collided, 1, axis=1), jnp.roll(collided, -1, axis=1), tables[4:6]
    )
    upper = jnp.concatenate(
        [read[..., NDIR:], jnp.zeros(read.shape[:2] + (NDIR,), jnp.float32)], axis=2
    )
    return (read + tables[6] * (upper - read)).reshape(rows, size)


def solution(mesh):
    in_specs = (P("space", "mom", None, None), P(None, "mom"), P(None, "mom"), P(), P())
    out_specs = P("space", "mom", None, None)

    return jax.shard_map(per_device, mesh=mesh, in_specs=in_specs, out_specs=out_specs, check_vma=False)
```

```python
import functools

import jax
import jax.numpy as jnp
from jax import lax
from jax.experimental import pallas as pl
from jax.experimental.pallas import tpu as pltpu
from jax.sharding import PartitionSpec as P


RANK = 8
NDIR = 16
ITERS = 2


collide_rate = 0.1
courant = 0.3


def swap(block, axis, bits):
    count = lax.axis_size(axis)
    return lax.ppermute(block, axis, [(i, i ^ bits) for i in range(count)])


def gathered(own, axis):
    count = lax.axis_size(axis)
    blocks = {0: own}
    for bits in range(4, count, 4):
        blocks[bits] = swap(own, axis, bits)
    for bits in range(0, count, 4):
        blocks[bits ^ 2] = swap(blocks[bits], axis, 2)
    return [blocks[2 * at] for at in range(count // 2)]


def off_chip(array):
    return pltpu.with_memory_space_constraint(array, pltpu.MemorySpace.HBM)


def prepare_kernel(
    state_hbm, velocity_hbm, drift_hbm, state_ref, rounded_ref, tables_ref, velocity_ref, drift_ref, sems
):
    copies = [
        pltpu.make_async_copy(source, target, sems.at[at])
        for at, (source, target) in enumerate(
            ((state_hbm, state_ref), (velocity_hbm, velocity_ref), (drift_hbm, drift_ref))
        )
    ]
    for copy in copies:
        copy.start()
    for copy in copies:
        copy.wait()
    rounded_ref[...] = state_ref[...].astype(jnp.bfloat16)
    for dim in range(3):
        speeds = velocity_ref[dim : dim + 1, :]
        tables_ref[2 * dim : 2 * dim + 1, :] = jnp.maximum(speeds, 0.0)
        tables_ref[2 * dim + 1 : 2 * dim + 2, :] = jnp.minimum(speeds, 0.0)
    tables_ref[6:7, :] = drift_ref[...]
    tables_ref[7:8, :] = drift_ref[...]


def prepare(state, velocity, drift):
    hbm = pl.BlockSpec(memory_space=pltpu.MemorySpace.HBM)
    whole = pl.BlockSpec(memory_space=pltpu.VMEM)
    return pl.pallas_call(
        prepare_kernel,
        out_shape=(
            jax.ShapeDtypeStruct(state.shape, jnp.float32),
            jax.ShapeDtypeStruct(state.shape, jnp.bfloat16),
            jax.ShapeDtypeStruct((8, state.shape[-1]), jnp.float32),
        ),
        in_specs=[hbm] * 3,
        out_specs=(whole,) * 3,
        scratch_shapes=[
            pltpu.VMEM(velocity.shape, jnp.float32),
            pltpu.VMEM((1, drift.shape[0]), jnp.float32),
            pltpu.SemaphoreType.DMA((3,)),
        ],
        compiler_params=pltpu.CompilerParams(vmem_limit_bytes=8 << 20),
        cost_estimate=pl.CostEstimate(
            flops=state.size, bytes_accessed=10 * state.size, transcendentals=0
        ),
    )(*[off_chip(each) for each in (state, velocity, drift.reshape(1, -1))])


def project(states, core, partner, own, copies):
    columns = partner[0].shape[1]
    width = columns // RANK
    step = min(columns, 256)
    total = jnp.zeros((states.shape[0], 2 * width), jnp.float32)
    for other, (a_ref, b_ref) in ((1, partner), (0, own)):
        if not other:
            for copy in copies:
                copy.wait()
        first = (core ^ other) * width
        for at in range(0, columns, step):
            proj_a = jnp.dot(states, a_ref[:, at : at + step], preferred_element_type=jnp.float32)
            proj_b = jnp.dot(states, b_ref[:, at : at + step], preferred_element_type=jnp.float32)
            product = proj_a * proj_b
            high = product.astype(jnp.bfloat16)
            low = (product - high.astype(jnp.float32)).astype(jnp.bfloat16)
            source = lax.broadcasted_iota(jnp.int32, (step, 2 * width), 0) + at
            target = lax.broadcasted_iota(jnp.int32, (step, 2 * width), 1)
            adds = jnp.where((source >> 3) + first == target, 1.0, 0.0).astype(jnp.bfloat16)
            total += jnp.dot(high, adds, preferred_element_type=jnp.float32)
            total += jnp.dot(low, adds, preferred_element_type=jnp.float32)
    return total


def fetches(factors, kept, sems):
    part = kept[0].shape[0] // sems.shape[1]
    copies = [
        pltpu.make_async_copy(
            source.at[at * part : (at + 1) * part],
            target.at[at * part : (at + 1) * part],
            sems.at[which, at],
        )
        for which, (source, target) in enumerate(zip(factors, kept))
        for at in range(sems.shape[1])
    ]
    for copy in copies:
        copy.start()
    return copies


def collide_kernel(chips, fetch, *refs):
    blocks, factors = refs[:chips], refs[chips : chips + 4]
    sent_ref, beside_ref = refs[chips + 4 : chips + 6]
    copies, kept = [], factors[:2]
    if fetch:
        kept = refs[chips + 6 : chips + 8]
        copies = fetches(factors[:2], kept, refs[chips + 8])
    me = lax.axis_index("mom")
    core, chip = me & 1, me >> 1
    rows = blocks[0].shape[0]
    states = jnp.concatenate([block[...] for block in blocks], axis=0)
    total = project(states, core, factors[2:], kept, copies)
    terms = total.astype(jnp.bfloat16)
    away = 2 * core - 1
    for at in range(chips):
        here = chip ^ at
        part = terms[at * rows : (at + 1) * rows]
        sent_ref[here, 0] = part
        sent_ref[(here + away) & (chips - 1), 1] = part

        @pl.when(here == ((chip - away) & (chips - 1)))
        def _():
            beside_ref[...] = blocks[at][...]


def collide(blocks, factors, fetch):
    chips, (rows, size) = len(blocks), blocks[0].shape
    columns = factors[0].shape[1]
    whole = pl.BlockSpec(memory_space=pltpu.VMEM)
    hbm = pl.BlockSpec(memory_space=pltpu.MemorySpace.HBM)
    factor = pltpu.VMEM((size, columns), jnp.bfloat16)
    return pl.pallas_call(
        functools.partial(collide_kernel, chips, fetch),
        out_shape=[
            jax.ShapeDtypeStruct((chips, 2, rows, 2 * columns // RANK), jnp.bfloat16),
            jax.ShapeDtypeStruct((rows, size), jnp.bfloat16),
        ],
        in_specs=[whole] * chips + [hbm if fetch else whole] * 2 + [whole] * 2,
        out_specs=[whole] * 2,
        scratch_shapes=[factor, factor, pltpu.SemaphoreType.DMA((2, 4))] if fetch else [],
        compiler_params=pltpu.CompilerParams(vmem_limit_bytes=16 << 20),
        cost_estimate=pl.CostEstimate(
            flops=8 * chips * rows * size * columns,
            bytes_accessed=2 * (chips * rows * size + 4 * size * columns),
            transcendentals=0,
        ),
    )(*blocks, *[off_chip(each) if fetch else each for each in factors[:2]], *factors[2:])


def keep_kernel(a_hbm, b_hbm, a_ref, b_ref, sems):
    for copy in fetches((a_hbm, b_hbm), (a_ref, b_ref), sems):
        copy.wait()


def keep(factors):
    hbm = pl.BlockSpec(memory_space=pltpu.MemorySpace.HBM)
    return pl.pallas_call(
        keep_kernel,
        out_shape=[jax.ShapeDtypeStruct(each.shape, each.dtype) for each in factors],
        in_specs=[hbm] * 2,
        out_specs=[pl.BlockSpec(memory_space=pltpu.VMEM)] * 2,
        scratch_shapes=[pltpu.SemaphoreType.DMA((2, 4))],
        compiler_params=pltpu.CompilerParams(vmem_limit_bytes=4 << 20),
        cost_estimate=pl.CostEstimate(
            flops=0, bytes_accessed=8 * factors[0].size, transcendentals=0
        ),
    )(*[off_chip(each) for each in factors])


def first_kernel(chips, layers, *refs):
    blocks, factors = refs[:chips], refs[chips : chips + 4]
    terms_ref, edges_ref = refs[chips + 4 :]
    me = lax.axis_index("mom")
    core, chip = me & 1, me >> 1
    rows = blocks[0].shape[0]
    depth = rows // layers
    states = jnp.concatenate([block[...] for block in blocks], axis=0)
    total = project(states, core, factors[2:], factors[:2], [])
    mine = total.shape[1]
    columns = pl.ds(pl.multiple_of(chip * mine, 128), mine)
    for at in range(chips):
        here = chip ^ at
        terms = total[at * rows : (at + 1) * rows].astype(jnp.bfloat16)
        terms_ref[here] = terms
        collided = blocks[at][:, columns].astype(jnp.float32)
        collided += collide_rate * terms.astype(jnp.float32)
        edges = jnp.concatenate([collided[rows - depth :], collided[:depth]], axis=0)
        edges_ref[here] = edges.astype(jnp.bfloat16)


def first_collision(blocks, factors, layers):
    chips, (rows, size) = len(blocks), blocks[0].shape
    columns = factors[0].shape[1]
    mine = 2 * columns // RANK
    return pl.pallas_call(
        functools.partial(first_kernel, chips, layers),
        out_shape=[
            jax.ShapeDtypeStruct((chips, rows, mine), jnp.bfloat16),
            jax.ShapeDtypeStruct((chips, 2 * rows // layers, mine), jnp.bfloat16),
        ],
        compiler_params=pltpu.CompilerParams(vmem_limit_bytes=16 << 20),
        cost_estimate=pl.CostEstimate(
            flops=8 * chips * rows * size * columns,
            bytes_accessed=2 * (chips * rows * size + 4 * size * columns),
            transcendentals=0,
        ),
    )(*blocks, *factors)


def collided_kernel(chips, rows, state_ref, *refs):
    blocks, parts = refs[:chips], refs[chips : 2 * chips]
    exact_ref, edges_ref, rounded_ref = refs[2 * chips :]
    chip = lax.axis_index("mom") >> 1
    mine = parts[0].shape[2]
    for source in range(chips):
        columns = pl.ds(pl.multiple_of((chip ^ source) * mine, 128), mine)
        for at in range(chips):
            here = chip ^ at
            part = parts[source][here].astype(jnp.float32)
            if at:
                state = blocks[at][:, columns].astype(jnp.float32)
            else:
                state = state_ref[:, columns]
            collided = state + collide_rate * part[:rows]
            exact_ref[here, :, columns] = collided
            rounded_ref[here, :, columns] = collided.astype(jnp.bfloat16)
            edges_ref[here, :, columns] = part[rows:]


def collided_cells(state, blocks, parts):
    chips, (rows, size) = len(blocks), blocks[0].shape
    edge = parts[0].shape[1] - rows
    return pl.pallas_call(
        functools.partial(collided_kernel, chips, rows),
        out_shape=[
            jax.ShapeDtypeStruct((chips, rows, size), jnp.float32),
            jax.ShapeDtypeStruct((chips, edge, size), jnp.float32),
            jax.ShapeDtypeStruct((chips, rows, size), jnp.bfloat16),
        ],
        compiler_params=pltpu.CompilerParams(vmem_limit_bytes=16 << 20),
        cost_estimate=pl.CostEstimate(
            flops=2 * chips * rows * size, bytes_accessed=10 * chips * rows * size, transcendentals=0
        ),
    )(state, *blocks, *parts)


def inner_kernel(layers, exact_ref, edges_ref, tables_ref, read_ref):
    chips, rows, size = exact_ref.shape
    depth = rows // layers

    @pl.loop(0, chips)
    def _(cell):
        for at in range(0, size, 128):
            lanes = slice(at, at + 128)
            center = exact_ref[cell, :, lanes]
            edges = edges_ref[cell, :, lanes]
            behind = jnp.concatenate([edges[:depth], center[: rows - depth]], axis=0)
            ahead = jnp.concatenate([center[depth:], edges[depth:]], axis=0)
            read = center - courant * upwind(center, behind, ahead, tables_ref[0:2, lanes])
            levels = center.reshape(layers, depth, 128)
            behind = pltpu.roll(levels, 1, 1).reshape(rows, 128)
            ahead = pltpu.roll(levels, depth - 1, 1).reshape(rows, 128)
            read = read - courant * upwind(center, behind, ahead, tables_ref[4:6, lanes])
            speeds = tables_ref[2:3, lanes] - tables_ref[3:4, lanes]
            read_ref[cell, :, lanes] = read - courant * speeds * center


def inner_update(exact, edges, tables, layers):
    return pl.pallas_call(
        functools.partial(inner_kernel, layers),
        out_shape=jax.ShapeDtypeStruct(exact.shape, jnp.float32),
        compiler_params=pltpu.CompilerParams(vmem_limit_bytes=8 << 20),
        cost_estimate=pl.CostEstimate(
            flops=20 * exact.size, bytes_accessed=8 * exact.size, transcendentals=0
        ),
    )(exact, edges, tables)


def drifted(read, after, drift):
    rolled = pltpu.roll(read, 128 - NDIR, 1)
    inside = lax.broadcasted_iota(jnp.int32, read.shape, 1) < 128 - NDIR
    upper = jnp.where(inside, rolled, 0.0 if after is None else after)
    return read + drift * (upper - read), rolled


def second_kernel(chips, inner_ref, other_ref, tables_ref, *refs):
    factors = refs[:4]
    sent_ref, own_ref, beside_ref, states_ref, updated_ref = refs[4:]
    me = lax.axis_index("mom")
    core, chip = me & 1, me >> 1
    away = 2 * core - 1
    _, rows, size = inner_ref.shape

    @pl.loop(0, chips)
    def _(cell):
        before, after = (cell - 1 + core) & (chips - 1), (cell + core) & (chips - 1)
        rolled = None
        for at in reversed(range(0, size, 128)):
            lanes = slice(at, at + 128)
            speeds = courant * tables_ref[2:4, lanes]
            read = inner_ref[cell, :, lanes]
            read += speeds[0:1] * other_ref[before, :, lanes].astype(jnp.float32)
            read -= speeds[1:2] * other_ref[after, :, lanes].astype(jnp.float32)
            state, rolled = drifted(read, rolled, tables_ref[6:7, lanes])
            states_ref[cell, :, lanes] = state.astype(jnp.bfloat16)
            updated_ref[cell, :, lanes] = state

    own_ref[...] = updated_ref[chip]
    beside_ref[...] = updated_ref[(chip - away) & (chips - 1)]
    states = states_ref[...].reshape(chips * rows, size)
    terms = project(states, core, factors[2:], factors[:2], []).astype(jnp.bfloat16)
    for here in range(chips):
        part = terms[here * rows : (here + 1) * rows]
        sent_ref[here, 0] = part
        sent_ref[(here + away) & (chips - 1), 1] = part


def second_collision(inner, other, tables, factors):
    chips, rows, size = inner.shape
    columns = factors[0].shape[1]
    return pl.pallas_call(
        functools.partial(second_kernel, chips),
        out_shape=[
            jax.ShapeDtypeStruct((chips, 2, rows, 2 * columns // RANK), jnp.bfloat16),
            jax.ShapeDtypeStruct((rows, size), jnp.float32),
            jax.ShapeDtypeStruct((rows, size), jnp.float32),
        ],
        scratch_shapes=[
            pltpu.VMEM((chips, rows, size), jnp.bfloat16),
            pltpu.VMEM((chips, rows, size), jnp.float32),
        ],
        compiler_params=pltpu.CompilerParams(vmem_limit_bytes=16 << 20),
        cost_estimate=pl.CostEstimate(
            flops=8 * chips * rows * size * columns,
            bytes_accessed=2 * (chips * rows * size + 4 * size * columns),
            transcendentals=0,
        ),
    )(inner, other, tables, *factors)


def arrive_kernel(layers, got_ref, own_ref, beside_ref, exact_ref, edges_ref, cells_ref):
    chips, _, rows, mine = got_ref.shape
    depth = rows // layers
    for source in range(chips):
        lanes = slice(source * mine, (source + 1) * mine)
        collided = own_ref[:, lanes] + collide_rate * got_ref[source, 0].astype(jnp.float32)
        beyond = beside_ref[:, lanes] + collide_rate * got_ref[source, 1].astype(jnp.float32)
        exact_ref[:, lanes] = collided
        edges = jnp.concatenate([collided[rows - depth :], collided[:depth]], axis=0)
        edges_ref[0, :, lanes] = edges.astype(jnp.bfloat16)
        cells_ref[0, :, lanes] = collided.astype(jnp.bfloat16)
        cells_ref[1, :, lanes] = beyond.astype(jnp.bfloat16)


def last_kernel(layers, exact_ref, edges_ref, cells_ref, tables_ref, out_ref):
    core = lax.axis_index("mom") & 1
    rows, size = exact_ref.shape
    depth = rows // layers
    rolled = None
    for at in reversed(range(0, size, 128)):
        lanes = slice(at, at + 128)
        center = exact_ref[:, lanes]
        edges = edges_ref[0, :, lanes].astype(jnp.float32)
        behind = jnp.concatenate([edges[:depth], center[: rows - depth]], axis=0)
        ahead = jnp.concatenate([center[depth:], edges[depth:]], axis=0)
        read = center - courant * upwind(center, behind, ahead, tables_ref[0:2, lanes])
        behind = cells_ref[1 - core, :, lanes].astype(jnp.float32)
        ahead = cells_ref[core, :, lanes].astype(jnp.float32)
        read = read - courant * upwind(center, behind, ahead, tables_ref[2:4, lanes])
        levels = center.reshape(layers, depth, 128)
        behind = pltpu.roll(levels, 1, 1).reshape(rows, 128)
        ahead = pltpu.roll(levels, depth - 1, 1).reshape(rows, 128)
        read = read - courant * upwind(center, behind, ahead, tables_ref[4:6, lanes])
        out_ref[:, lanes], rolled = drifted(read, rolled, tables_ref[6:7, lanes])


def settled(state, sent, beside, tables, layers):
    rows, size = state.shape
    chips = sent.shape[0]
    same = [[c + 2 * k for k in range(chips)] for c in range(2)]
    got = lax.all_to_all(
        sent, "mom", split_axis=0, concat_axis=0, tiled=True, axis_index_groups=same
    )
    params = pltpu.CompilerParams(vmem_limit_bytes=4 << 20)
    cost = pl.CostEstimate(flops=20 * state.size, bytes_accessed=12 * state.size, transcendentals=0)
    exact, edges, cells = pl.pallas_call(
        functools.partial(arrive_kernel, layers),
        out_shape=[
            jax.ShapeDtypeStruct((rows, size), jnp.float32),
            jax.ShapeDtypeStruct((1, 2 * rows // layers, size), jnp.bfloat16),
            jax.ShapeDtypeStruct((2, rows, size), jnp.bfloat16),
        ],
        compiler_params=params,
        cost_estimate=cost,
    )(got, state, beside)
    edges = edge_layers(edges, "space")
    cells = swap(cells, "mom", 1)
    return pl.pallas_call(
        functools.partial(last_kernel, layers),
        out_shape=jax.ShapeDtypeStruct((rows, size), jnp.float32),
        compiler_params=params,
        cost_estimate=cost,
    )(exact, edges, cells, tables)


def edge_layers(edges, axis):
    count = lax.axis_size(axis)
    if count == 2:
        return swap(edges, axis, 1)
    depth = edges.shape[1] // 2
    last, first = edges[:, :depth], edges[:, depth:]
    behind = lax.ppermute(last, axis, [(i, (i + 1) % count) for i in range(count)])
    ahead = lax.ppermute(first, axis, [((i + 1) % count, i) for i in range(count)])
    return jnp.concatenate([behind, ahead], axis=1)


def x_halo(cells, axis, dtype):
    count = lax.axis_size(axis)
    size = cells.shape[0]
    head = cells[:1].astype(dtype)
    tail = cells[size - 1 :].astype(dtype)
    if count == 2:
        both = swap(jnp.concatenate([tail, head], axis=0), axis, 1)
        behind, ahead = both[:1], both[1:]
    else:
        behind = lax.ppermute(tail, axis, [(i, (i + 1) % count) for i in range(count)])
        ahead = lax.ppermute(head, axis, [((i + 1) % count, i) for i in range(count)])
    return behind.astype(cells.dtype), ahead.astype(cells.dtype)


def upwind(center, behind, beyond, speeds):
    return speeds[0:1] * (center - behind) + speeds[1:2] * (beyond - center)


def per_device(distribution, a_factor, b_factor, velocity, drift):
    layers, owned, depth, size = distribution.shape
    assert owned == 1
    partner = (swap(a_factor, "mom", 1), swap(b_factor, "mom", 1))
    factors = (a_factor, b_factor, *partner)
    state, rounded, tables = prepare(distribution.reshape(layers * depth, size), velocity, drift)
    if 2 * (a_factor.shape[1] // RANK) % 128:
        for substep in range(ITERS):
            sent, beside = collide(gathered(rounded, "mom"), factors, substep == 0)
            state = settle(state, sent, beside.astype(jnp.float32), tables, layers)
            rounded = state.astype(jnp.bfloat16)
        return state.reshape(distribution.shape)
    factors = (*keep((a_factor, b_factor)), *partner)
    for _ in range(0, ITERS, 2):
        blocks = gathered(rounded, "mom")
        terms, edges = first_collision(blocks, factors, layers)
        parts = gathered(jnp.concatenate([terms, edge_layers(edges, "space")], axis=1), "mom")
        exact, edges, cells = collided_cells(state, blocks, parts)
        other = swap(cells, "mom", 1)
        inner = inner_update(exact, edges, tables, layers)
        sent, state, beside = second_collision(inner, other, tables, factors)
        state = settled(state, sent, beside, tables, layers)
        rounded = state.astype(jnp.bfloat16)
    return state.reshape(distribution.shape)


def settle(state, sent, beside, tables, layers):
    rows, size = state.shape
    shape = (layers, rows // layers, size)
    chips = sent.shape[0]
    odd = lax.axis_index("mom") % 2 == 1
    same = [[c + 2 * k for k in range(chips)] for c in range(2)]
    got = lax.all_to_all(
        sent, "mom", split_axis=0, concat_axis=0, tiled=True, axis_index_groups=same
    )
    got = jnp.moveaxis(got, 0, 2).reshape((2,) + shape).astype(jnp.float32)
    collided = state.reshape(shape) + collide_rate * got[0]
    beside = beside.reshape(shape) + collide_rate * got[1]
    x_behind, x_ahead = x_halo(collided, "space", jnp.bfloat16)
    near, far = swap(jnp.stack([collided, beside]).astype(jnp.bfloat16), "mom", 1).astype(
        jnp.float32
    )
    y_behind = jnp.where(odd, near, far)
    y_ahead = jnp.where(odd, far, near)
    x_behind = jnp.concatenate([x_behind, collided[:-1]], axis=0)
    x_ahead = jnp.concatenate([collided[1:], x_ahead], axis=0)
    read = collided - courant * upwind(collided, x_behind, x_ahead, tables[0:2])
    read = read - courant * upwind(collided, y_behind, y_ahead, tables[2:4])
    read = read - courant * upwind(
        collided, jnp.roll(collided, 1, axis=1), jnp.roll(collided, -1, axis=1), tables[4:6]
    )
    upper = jnp.concatenate(
        [read[..., NDIR:], jnp.zeros(read.shape[:2] + (NDIR,), jnp.float32)], axis=2
    )
    return (read + tables[6] * (upper - read)).reshape(rows, size)


def solution(mesh):
    in_specs = (P("space", "mom", None, None), P(None, "mom"), P(None, "mom"), P(), P())
    out_specs = P("space", "mom", None, None)

    return jax.shard_map(per_device, mesh=mesh, in_specs=in_specs, out_specs=out_specs, check_vma=False)
```

```python
import functools

import jax
import jax.numpy as jnp
from jax import lax
from jax.experimental import pallas as pl
from jax.experimental.pallas import tpu as pltpu
from jax.sharding import PartitionSpec as P


RANK = 8
NDIR = 16
ITERS = 2


collide_rate = 0.1
courant = 0.3


def swap(block, axis, bits):
    count = lax.axis_size(axis)
    return lax.ppermute(block, axis, [(i, i ^ bits) for i in range(count)])


def gathered(own, axis):
    count = lax.axis_size(axis)
    blocks = {0: own}
    for bits in range(4, count, 4):
        blocks[bits] = swap(own, axis, bits)
    for bits in range(0, count, 4):
        blocks[bits ^ 2] = swap(blocks[bits], axis, 2)
    return [blocks[2 * at] for at in range(count // 2)]


def off_chip(array):
    return pltpu.with_memory_space_constraint(array, pltpu.MemorySpace.HBM)


def prepare_kernel(
    state_hbm, velocity_hbm, drift_hbm, state_ref, rounded_ref, tables_ref, velocity_ref, drift_ref, sems
):
    copies = [
        pltpu.make_async_copy(source, target, sems.at[at])
        for at, (source, target) in enumerate(
            ((state_hbm, state_ref), (velocity_hbm, velocity_ref), (drift_hbm, drift_ref))
        )
    ]
    for copy in copies:
        copy.start()
    for copy in copies:
        copy.wait()
    rounded_ref[...] = state_ref[...].astype(jnp.bfloat16)
    for dim in range(3):
        speeds = velocity_ref[dim : dim + 1, :]
        tables_ref[2 * dim : 2 * dim + 1, :] = jnp.maximum(speeds, 0.0)
        tables_ref[2 * dim + 1 : 2 * dim + 2, :] = jnp.minimum(speeds, 0.0)
    tables_ref[6:7, :] = drift_ref[...]
    tables_ref[7:8, :] = drift_ref[...]


def prepare(state, velocity, drift):
    hbm = pl.BlockSpec(memory_space=pltpu.MemorySpace.HBM)
    whole = pl.BlockSpec(memory_space=pltpu.VMEM)
    return pl.pallas_call(
        prepare_kernel,
        out_shape=(
            jax.ShapeDtypeStruct(state.shape, jnp.float32),
            jax.ShapeDtypeStruct(state.shape, jnp.bfloat16),
            jax.ShapeDtypeStruct((8, state.shape[-1]), jnp.float32),
        ),
        in_specs=[hbm] * 3,
        out_specs=(whole,) * 3,
        scratch_shapes=[
            pltpu.VMEM(velocity.shape, jnp.float32),
            pltpu.VMEM((1, drift.shape[0]), jnp.float32),
            pltpu.SemaphoreType.DMA((3,)),
        ],
        compiler_params=pltpu.CompilerParams(vmem_limit_bytes=8 << 20),
        cost_estimate=pl.CostEstimate(
            flops=state.size, bytes_accessed=10 * state.size, transcendentals=0
        ),
    )(*[off_chip(each) for each in (state, velocity, drift.reshape(1, -1))])


def project(states, core, partner, own, copies):
    columns = partner[0].shape[1]
    width = columns // RANK
    step = min(columns, 512)
    total = jnp.zeros((states.shape[0], 2 * width), jnp.float32)
    for other, (a_ref, b_ref) in ((1, partner), (0, own)):
        if not other:
            for copy in copies:
                copy.wait()
        first = (core ^ other) * width
        for at in range(0, columns, step):
            proj_a = jnp.dot(states, a_ref[:, at : at + step], preferred_element_type=jnp.float32)
            proj_b = jnp.dot(states, b_ref[:, at : at + step], preferred_element_type=jnp.float32)
            product = proj_a * proj_b
            high = product.astype(jnp.bfloat16)
            low = (product - high.astype(jnp.float32)).astype(jnp.bfloat16)
            source = lax.broadcasted_iota(jnp.int32, (step, 2 * width), 0) + at
            target = lax.broadcasted_iota(jnp.int32, (step, 2 * width), 1)
            adds = jnp.where((source >> 3) + first == target, 1.0, 0.0).astype(jnp.bfloat16)
            split = jnp.concatenate([high, low], axis=1)
            twice = jnp.concatenate([adds, adds], axis=0)
            total += jnp.dot(split, twice, preferred_element_type=jnp.float32)
    return total


def fetches(factors, kept, sems):
    part = kept[0].shape[0] // sems.shape[1]
    copies = [
        pltpu.make_async_copy(
            source.at[at * part : (at + 1) * part],
            target.at[at * part : (at + 1) * part],
            sems.at[which, at],
        )
        for which, (source, target) in enumerate(zip(factors, kept))
        for at in range(sems.shape[1])
    ]
    for copy in copies:
        copy.start()
    return copies


def collide_kernel(chips, fetch, *refs):
    blocks, factors = refs[:chips], refs[chips : chips + 4]
    sent_ref, beside_ref = refs[chips + 4 : chips + 6]
    copies, kept = [], factors[:2]
    if fetch:
        kept = refs[chips + 6 : chips + 8]
        copies = fetches(factors[:2], kept, refs[chips + 8])
    me = lax.axis_index("mom")
    core, chip = me & 1, me >> 1
    rows = blocks[0].shape[0]
    states = jnp.concatenate([block[...] for block in blocks], axis=0)
    total = project(states, core, factors[2:], kept, copies)
    terms = total.astype(jnp.bfloat16)
    away = 2 * core - 1
    for at in range(chips):
        here = chip ^ at
        part = terms[at * rows : (at + 1) * rows]
        sent_ref[here, 0] = part
        sent_ref[(here + away) & (chips - 1), 1] = part

        @pl.when(here == ((chip - away) & (chips - 1)))
        def _():
            beside_ref[...] = blocks[at][...]


def collide(blocks, factors, fetch):
    chips, (rows, size) = len(blocks), blocks[0].shape
    columns = factors[0].shape[1]
    whole = pl.BlockSpec(memory_space=pltpu.VMEM)
    hbm = pl.BlockSpec(memory_space=pltpu.MemorySpace.HBM)
    factor = pltpu.VMEM((size, columns), jnp.bfloat16)
    return pl.pallas_call(
        functools.partial(collide_kernel, chips, fetch),
        out_shape=[
            jax.ShapeDtypeStruct((chips, 2, rows, 2 * columns // RANK), jnp.bfloat16),
            jax.ShapeDtypeStruct((rows, size), jnp.bfloat16),
        ],
        in_specs=[whole] * chips + [hbm if fetch else whole] * 2 + [whole] * 2,
        out_specs=[whole] * 2,
        scratch_shapes=[factor, factor, pltpu.SemaphoreType.DMA((2, 4))] if fetch else [],
        compiler_params=pltpu.CompilerParams(vmem_limit_bytes=16 << 20),
        cost_estimate=pl.CostEstimate(
            flops=8 * chips * rows * size * columns,
            bytes_accessed=2 * (chips * rows * size + 4 * size * columns),
            transcendentals=0,
        ),
    )(*blocks, *[off_chip(each) if fetch else each for each in factors[:2]], *factors[2:])


def keep_kernel(a_hbm, b_hbm, a_ref, b_ref, sems):
    for copy in fetches((a_hbm, b_hbm), (a_ref, b_ref), sems):
        copy.wait()


def keep(factors):
    hbm = pl.BlockSpec(memory_space=pltpu.MemorySpace.HBM)
    return pl.pallas_call(
        keep_kernel,
        out_shape=[jax.ShapeDtypeStruct(each.shape, each.dtype) for each in factors],
        in_specs=[hbm] * 2,
        out_specs=[pl.BlockSpec(memory_space=pltpu.VMEM)] * 2,
        scratch_shapes=[pltpu.SemaphoreType.DMA((2, 4))],
        compiler_params=pltpu.CompilerParams(vmem_limit_bytes=4 << 20),
        cost_estimate=pl.CostEstimate(
            flops=0, bytes_accessed=8 * factors[0].size, transcendentals=0
        ),
    )(*[off_chip(each) for each in factors])


def first_kernel(chips, layers, *refs):
    blocks, factors = refs[:chips], refs[chips : chips + 4]
    terms_ref, edges_ref = refs[chips + 4 :]
    me = lax.axis_index("mom")
    core, chip = me & 1, me >> 1
    rows = blocks[0].shape[0]
    depth = rows // layers
    states = jnp.concatenate([block[...] for block in blocks], axis=0)
    total = project(states, core, factors[2:], factors[:2], [])
    mine = total.shape[1]
    columns = pl.ds(pl.multiple_of(chip * mine, 128), mine)
    for at in range(chips):
        here = chip ^ at
        terms = total[at * rows : (at + 1) * rows].astype(jnp.bfloat16)
        terms_ref[here] = terms
        collided = blocks[at][:, columns].astype(jnp.float32)
        collided += collide_rate * terms.astype(jnp.float32)
        edges = jnp.concatenate([collided[rows - depth :], collided[:depth]], axis=0)
        edges_ref[here] = edges.astype(jnp.bfloat16)


def first_collision(blocks, factors, layers):
    chips, (rows, size) = len(blocks), blocks[0].shape
    columns = factors[0].shape[1]
    mine = 2 * columns // RANK
    return pl.pallas_call(
        functools.partial(first_kernel, chips, layers),
        out_shape=[
            jax.ShapeDtypeStruct((chips, rows, mine), jnp.bfloat16),
            jax.ShapeDtypeStruct((chips, 2 * rows // layers, mine), jnp.bfloat16),
        ],
        compiler_params=pltpu.CompilerParams(vmem_limit_bytes=16 << 20),
        cost_estimate=pl.CostEstimate(
            flops=8 * chips * rows * size * columns,
            bytes_accessed=2 * (chips * rows * size + 4 * size * columns),
            transcendentals=0,
        ),
    )(*blocks, *factors)


def collided_kernel(chips, rows, state_ref, *refs):
    blocks, parts = refs[:chips], refs[chips : 2 * chips]
    exact_ref, edges_ref, rounded_ref = refs[2 * chips :]
    chip = lax.axis_index("mom") >> 1
    mine = parts[0].shape[2]
    for source in range(chips):
        columns = pl.ds(pl.multiple_of((chip ^ source) * mine, 128), mine)
        for at in range(chips):
            here = chip ^ at
            part = parts[source][here].astype(jnp.float32)
            if at:
                state = blocks[at][:, columns].astype(jnp.float32)
            else:
                state = state_ref[:, columns]
            collided = state + collide_rate * part[:rows]
            exact_ref[here, :, columns] = collided
            rounded_ref[here, :, columns] = collided.astype(jnp.bfloat16)
            edges_ref[here, :, columns] = part[rows:]


def collided_cells(state, blocks, parts):
    chips, (rows, size) = len(blocks), blocks[0].shape
    edge = parts[0].shape[1] - rows
    return pl.pallas_call(
        functools.partial(collided_kernel, chips, rows),
        out_shape=[
            jax.ShapeDtypeStruct((chips, rows, size), jnp.float32),
            jax.ShapeDtypeStruct((chips, edge, size), jnp.float32),
            jax.ShapeDtypeStruct((chips, rows, size), jnp.bfloat16),
        ],
        compiler_params=pltpu.CompilerParams(vmem_limit_bytes=16 << 20),
        cost_estimate=pl.CostEstimate(
            flops=2 * chips * rows * size, bytes_accessed=10 * chips * rows * size, transcendentals=0
        ),
    )(state, *blocks, *parts)


def inner_kernel(layers, exact_ref, edges_ref, tables_ref, read_ref):
    chips, rows, size = exact_ref.shape
    depth = rows // layers

    @pl.loop(0, chips, unroll=True)
    def _(cell):
        for at in range(0, size, 128):
            lanes = slice(at, at + 128)
            center = exact_ref[cell, :, lanes]
            edges = edges_ref[cell, :, lanes]
            behind = jnp.concatenate([edges[:depth], center[: rows - depth]], axis=0)
            ahead = jnp.concatenate([center[depth:], edges[depth:]], axis=0)
            read = center - courant * upwind(center, behind, ahead, tables_ref[0:2, lanes])
            levels = center.reshape(layers, depth, 128)
            behind = pltpu.roll(levels, 1, 1).reshape(rows, 128)
            ahead = pltpu.roll(levels, depth - 1, 1).reshape(rows, 128)
            read = read - courant * upwind(center, behind, ahead, tables_ref[4:6, lanes])
            speeds = tables_ref[2:3, lanes] - tables_ref[3:4, lanes]
            read_ref[cell, :, lanes] = read - courant * speeds * center


def inner_update(exact, edges, tables, layers):
    return pl.pallas_call(
        functools.partial(inner_kernel, layers),
        out_shape=jax.ShapeDtypeStruct(exact.shape, jnp.float32),
        compiler_params=pltpu.CompilerParams(vmem_limit_bytes=8 << 20),
        cost_estimate=pl.CostEstimate(
            flops=20 * exact.size, bytes_accessed=8 * exact.size, transcendentals=0
        ),
    )(exact, edges, tables)


def drifted(read, after, drift):
    rolled = pltpu.roll(read, 128 - NDIR, 1)
    inside = lax.broadcasted_iota(jnp.int32, read.shape, 1) < 128 - NDIR
    upper = jnp.where(inside, rolled, 0.0 if after is None else after)
    return read + drift * (upper - read), rolled


def second_kernel(chips, inner_ref, other_ref, tables_ref, *refs):
    factors = refs[:4]
    sent_ref, own_ref, beside_ref, states_ref, updated_ref = refs[4:]
    me = lax.axis_index("mom")
    core, chip = me & 1, me >> 1
    away = 2 * core - 1
    _, rows, size = inner_ref.shape

    @pl.loop(0, chips, unroll=True)
    def _(cell):
        before, after = (cell - 1 + core) & (chips - 1), (cell + core) & (chips - 1)
        rolled = None
        for at in reversed(range(0, size, 128)):
            lanes = slice(at, at + 128)
            speeds = courant * tables_ref[2:4, lanes]
            read = inner_ref[cell, :, lanes]
            read += speeds[0:1] * other_ref[before, :, lanes].astype(jnp.float32)
            read -= speeds[1:2] * other_ref[after, :, lanes].astype(jnp.float32)
            state, rolled = drifted(read, rolled, tables_ref[6:7, lanes])
            states_ref[cell, :, lanes] = state.astype(jnp.bfloat16)
            updated_ref[cell, :, lanes] = state

    own_ref[...] = updated_ref[chip]
    beside_ref[...] = updated_ref[(chip - away) & (chips - 1)]
    states = states_ref[...].reshape(chips * rows, size)
    terms = project(states, core, factors[2:], factors[:2], []).astype(jnp.bfloat16)
    for here in range(chips):
        part = terms[here * rows : (here + 1) * rows]
        sent_ref[here, 0] = part
        sent_ref[(here + away) & (chips - 1), 1] = part


def second_collision(inner, other, tables, factors):
    chips, rows, size = inner.shape
    columns = factors[0].shape[1]
    return pl.pallas_call(
        functools.partial(second_kernel, chips),
        out_shape=[
            jax.ShapeDtypeStruct((chips, 2, rows, 2 * columns // RANK), jnp.bfloat16),
            jax.ShapeDtypeStruct((rows, size), jnp.float32),
            jax.ShapeDtypeStruct((rows, size), jnp.float32),
        ],
        scratch_shapes=[
            pltpu.VMEM((chips, rows, size), jnp.bfloat16),
            pltpu.VMEM((chips, rows, size), jnp.float32),
        ],
        compiler_params=pltpu.CompilerParams(vmem_limit_bytes=16 << 20),
        cost_estimate=pl.CostEstimate(
            flops=8 * chips * rows * size * columns,
            bytes_accessed=2 * (chips * rows * size + 4 * size * columns),
            transcendentals=0,
        ),
    )(inner, other, tables, *factors)


def arrive_kernel(layers, got_ref, own_ref, beside_ref, exact_ref, edges_ref, cells_ref):
    chips, _, rows, mine = got_ref.shape
    depth = rows // layers
    for source in range(chips):
        lanes = slice(source * mine, (source + 1) * mine)
        collided = own_ref[:, lanes] + collide_rate * got_ref[source, 0].astype(jnp.float32)
        beyond = beside_ref[:, lanes] + collide_rate * got_ref[source, 1].astype(jnp.float32)
        exact_ref[:, lanes] = collided
        edges = jnp.concatenate([collided[rows - depth :], collided[:depth]], axis=0)
        edges_ref[0, :, lanes] = edges.astype(jnp.bfloat16)
        cells_ref[0, :, lanes] = collided.astype(jnp.bfloat16)
        cells_ref[1, :, lanes] = beyond.astype(jnp.bfloat16)


def last_kernel(layers, exact_ref, edges_ref, cells_ref, tables_ref, out_ref):
    core = lax.axis_index("mom") & 1
    rows, size = exact_ref.shape
    depth = rows // layers
    rolled = None
    for at in reversed(range(0, size, 128)):
        lanes = slice(at, at + 128)
        center = exact_ref[:, lanes]
        edges = edges_ref[0, :, lanes].astype(jnp.float32)
        behind = jnp.concatenate([edges[:depth], center[: rows - depth]], axis=0)
        ahead = jnp.concatenate([center[depth:], edges[depth:]], axis=0)
        read = center - courant * upwind(center, behind, ahead, tables_ref[0:2, lanes])
        behind = cells_ref[1 - core, :, lanes].astype(jnp.float32)
        ahead = cells_ref[core, :, lanes].astype(jnp.float32)
        read = read - courant * upwind(center, behind, ahead, tables_ref[2:4, lanes])
        levels = center.reshape(layers, depth, 128)
        behind = pltpu.roll(levels, 1, 1).reshape(rows, 128)
        ahead = pltpu.roll(levels, depth - 1, 1).reshape(rows, 128)
        read = read - courant * upwind(center, behind, ahead, tables_ref[4:6, lanes])
        out_ref[:, lanes], rolled = drifted(read, rolled, tables_ref[6:7, lanes])


def settled(state, sent, beside, tables, layers):
    rows, size = state.shape
    chips = sent.shape[0]
    same = [[c + 2 * k for k in range(chips)] for c in range(2)]
    got = lax.all_to_all(
        sent, "mom", split_axis=0, concat_axis=0, tiled=True, axis_index_groups=same
    )
    params = pltpu.CompilerParams(vmem_limit_bytes=4 << 20)
    cost = pl.CostEstimate(flops=20 * state.size, bytes_accessed=12 * state.size, transcendentals=0)
    exact, edges, cells = pl.pallas_call(
        functools.partial(arrive_kernel, layers),
        out_shape=[
            jax.ShapeDtypeStruct((rows, size), jnp.float32),
            jax.ShapeDtypeStruct((1, 2 * rows // layers, size), jnp.bfloat16),
            jax.ShapeDtypeStruct((2, rows, size), jnp.bfloat16),
        ],
        compiler_params=params,
        cost_estimate=cost,
    )(got, state, beside)
    edges = edge_layers(edges, "space")
    cells = swap(cells, "mom", 1)
    return pl.pallas_call(
        functools.partial(last_kernel, layers),
        out_shape=jax.ShapeDtypeStruct((rows, size), jnp.float32),
        compiler_params=params,
        cost_estimate=cost,
    )(exact, edges, cells, tables)


def edge_layers(edges, axis):
    count = lax.axis_size(axis)
    if count == 2:
        return swap(edges, axis, 1)
    depth = edges.shape[1] // 2
    last, first = edges[:, :depth], edges[:, depth:]
    behind = lax.ppermute(last, axis, [(i, (i + 1) % count) for i in range(count)])
    ahead = lax.ppermute(first, axis, [((i + 1) % count, i) for i in range(count)])
    return jnp.concatenate([behind, ahead], axis=1)


def x_halo(cells, axis, dtype):
    count = lax.axis_size(axis)
    size = cells.shape[0]
    head = cells[:1].astype(dtype)
    tail = cells[size - 1 :].astype(dtype)
    if count == 2:
        both = swap(jnp.concatenate([tail, head], axis=0), axis, 1)
        behind, ahead = both[:1], both[1:]
    else:
        behind = lax.ppermute(tail, axis, [(i, (i + 1) % count) for i in range(count)])
        ahead = lax.ppermute(head, axis, [((i + 1) % count, i) for i in range(count)])
    return behind.astype(cells.dtype), ahead.astype(cells.dtype)


def upwind(center, behind, beyond, speeds):
    return speeds[0:1] * (center - behind) + speeds[1:2] * (beyond - center)


def per_device(distribution, a_factor, b_factor, velocity, drift):
    layers, owned, depth, size = distribution.shape
    assert owned == 1
    partner = (swap(a_factor, "mom", 1), swap(b_factor, "mom", 1))
    factors = (a_factor, b_factor, *partner)
    state, rounded, tables = prepare(distribution.reshape(layers * depth, size), velocity, drift)
    if 2 * (a_factor.shape[1] // RANK) % 128:
        for substep in range(ITERS):
            sent, beside = collide(gathered(rounded, "mom"), factors, substep == 0)
            state = settle(state, sent, beside.astype(jnp.float32), tables, layers)
            rounded = state.astype(jnp.bfloat16)
        return state.reshape(distribution.shape)
    factors = (*keep((a_factor, b_factor)), *partner)
    for _ in range(0, ITERS, 2):
        blocks = gathered(rounded, "mom")
        terms, edges = first_collision(blocks, factors, layers)
        parts = gathered(jnp.concatenate([terms, edge_layers(edges, "space")], axis=1), "mom")
        exact, edges, cells = collided_cells(state, blocks, parts)
        other = swap(cells, "mom", 1)
        inner = inner_update(exact, edges, tables, layers)
        sent, state, beside = second_collision(inner, other, tables, factors)
        state = settled(state, sent, beside, tables, layers)
        rounded = state.astype(jnp.bfloat16)
    return state.reshape(distribution.shape)


def settle(state, sent, beside, tables, layers):
    rows, size = state.shape
    shape = (layers, rows // layers, size)
    chips = sent.shape[0]
    odd = lax.axis_index("mom") % 2 == 1
    same = [[c + 2 * k for k in range(chips)] for c in range(2)]
    got = lax.all_to_all(
        sent, "mom", split_axis=0, concat_axis=0, tiled=True, axis_index_groups=same
    )
    got = jnp.moveaxis(got, 0, 2).reshape((2,) + shape).astype(jnp.float32)
    collided = state.reshape(shape) + collide_rate * got[0]
    beside = beside.reshape(shape) + collide_rate * got[1]
    x_behind, x_ahead = x_halo(collided, "space", jnp.bfloat16)
    near, far = swap(jnp.stack([collided, beside]).astype(jnp.bfloat16), "mom", 1).astype(
        jnp.float32
    )
    y_behind = jnp.where(odd, near, far)
    y_ahead = jnp.where(odd, far, near)
    x_behind = jnp.concatenate([x_behind, collided[:-1]], axis=0)
    x_ahead = jnp.concatenate([collided[1:], x_ahead], axis=0)
    read = collided - courant * upwind(collided, x_behind, x_ahead, tables[0:2])
    read = read - courant * upwind(collided, y_behind, y_ahead, tables[2:4])
    read = read - courant * upwind(
        collided, jnp.roll(collided, 1, axis=1), jnp.roll(collided, -1, axis=1), tables[4:6]
    )
    upper = jnp.concatenate(
        [read[..., NDIR:], jnp.zeros(read.shape[:2] + (NDIR,), jnp.float32)], axis=2
    )
    return (read + tables[6] * (upper - read)).reshape(rows, size)


def solution(mesh):
    in_specs = (P("space", "mom", None, None), P(None, "mom"), P(None, "mom"), P(), P())
    out_specs = P("space", "mom", None, None)

    return jax.shard_map(per_device, mesh=mesh, in_specs=in_specs, out_specs=out_specs, check_vma=False)
```
